32 devices in a mesh: segment: 2 (over x), expert: 16 (over z, y, core).
Axes of the slice: x: 2, y: 2, z: 4, core: 2. Of those that a mesh axis runs over, the one named last changes fastest.
Arguments:
- handoff: bfloat16 [2, 1024, 4096], P('segment', 'expert'), may hold values from -6 to 6
- saved_inputs: bfloat16 [2, 1024, 4096], P('segment', 'expert'), may hold values from -6 to 6
- cotangent: bfloat16 [2, 1024, 4096], P('segment', 'expert'), may hold values from -6 to 6
- ids_forward: int32 [2, 1024, 2], P('segment', 'expert'), may hold values from 0 to 63, all different within a row; in each aligned block of 64 rows (0 to 63, 64 to 127, ..., all dimensions but the last counted through in order) at most 5 rows name the same one
- gates_forward: float32 [2, 1024, 2], P('segment', 'expert'), may hold values from 0.25 to 1
- ids_backward: int32 [2, 1024, 2], P('segment', 'expert'), may hold values from 0 to 63, all different within a row; in each aligned block of 64 rows (0 to 63, 64 to 127, ..., all dimensions but the last counted through in order) at most 5 rows name the same one
- gates_backward: float32 [2, 1024, 2], P('segment', 'expert'), may hold values from 0.25 to 1
- weight_in: bfloat16 [2, 4096, 2048], P('segment', None, 'expert'), may hold values from -0.09375 to 0.09375
- weight_out: bfloat16 [2, 2048, 4096], P('segment', 'expert'), may hold values from -0.125 to 0.125
Outputs:
- expert_mix: bfloat16 [2, 1024, 4096], P('segment', 'expert')
- input_grads: bfloat16 [2, 1024, 4096], P('segment', 'expert')
The draws below stay inside these ranges and needn't reach their ends.
Inputs may be any that keep to these rules, and one draw needn't show every extreme that they name: `ids_forward`: the two experts of a row differ; within the rows of one device no expert is named by more than 5 rows. `ids_backward`: the two experts of a row differ; within the rows of one device no expert is named by more than 5 rows.
All inputs are finite; a program needn't handle non-finite values.
Results may differ from the reference program's by a relative error of at most 0.013.
Values may be sent and summed in bfloat16 or wider, within the bound.
A program may use at most 128 MiB of HBM per device.

```python
import math
from functools import partial
import jax
import jax.numpy as jnp
import numpy as np
from jax import lax

D = 4096
FF = 2048
ALL_EXPERTS = 64
GROUP = 16
ROWS_DEV = 64
CAP = 5
EXPERTS = 1
ROWS = 1024
SEGMENTS = 2
N_EXPERT = 16


def levels(own_key, extent, shards, low, high):
    def one(dim, shards_of):
        draws = jax.random.uniform(jax.random.fold_in(jax.random.fold_in(own_key, 6), dim), (shards_of,), jnp.float32, low / len(shards), high / len(shards))
        return jnp.repeat(jnp.exp(draws), extent[dim] // shards_of).reshape((-1,) + (1,) * (len(extent) - dim - 1))

    factor_of = one(*shards[0])
    for cut in shards[1:]:
        factor_of = factor_of * one(*cut)
    return factor_of


def deal_out(key, own, number, rows, number_of, top, reach, slope):
    ranking = jax.random.permutation(key, number_of)
    heavy_load, common = portions_of(number_of, rows * top, reach, slope, True), portions_of(number_of, rows * top, reach, slope, False)
    places = jnp.arange(number_of)

    def named(tallies, offset_by):
        used = int((tallies > 0).sum())
        fixed = max(1, used // 4)
        moved = fixed + (places - fixed + offset_by * (used - fixed)) % max(1, number_of - fixed)
        return jnp.zeros((number_of,), jnp.int32).at[ranking[jnp.where(places < fixed, places, moved)]].set(jnp.asarray(tallies, jnp.int32))

    tallies = jnp.where(number % 4 == 0, named(heavy_load, number // 4), named(common, number - number // 4 - 1))
    mixed = jax.random.permutation(jax.random.fold_in(own, 3), number_of)
    source_of, sink = mixed[0:number_of // 2 * 2:2], mixed[1:number_of // 2 * 2:2]
    slack = jnp.minimum(tallies[source_of] - 1, reach - tallies[sink]) // 2
    slack = jnp.where((source_of == ranking[0]) | (sink == ranking[0]) | (tallies[sink] == 0), 0, jnp.maximum(slack, 0))
    moved = jax.random.randint(jax.random.fold_in(own, 4), (number_of // 2,), 0, 1 << 20) % (slack + 1)
    tallies = tallies.at[source_of].add(-moved).at[sink].add(moved)
    labels = jnp.searchsorted(jnp.cumsum(tallies), jnp.arange(rows * top), side="right").astype(jnp.int32)
    table = labels.reshape(top, rows).T
    table = table[jax.random.permutation(jax.random.fold_in(own, 1), rows)]
    offset_by = jax.random.randint(jax.random.fold_in(own, 2), (rows, 1), 0, top)
    return jnp.take_along_axis(table, (jnp.arange(top)[None, :] + offset_by) % top, axis=1)


def portions_of(count, total, limit, skew, full):
    portions = [(1 << 20) // math.isqrt(rank ** skew) + 1 for rank in range(1, count + 1)]
    largest = limit if full else min(limit, max(-(-total // count), total * portions[0] // sum(portions)))
    least = 1 if total - largest >= count - 1 else 0
    counts, spare = [largest] + [least] * (count - 1), total - largest - least * (count - 1)
    while spare > 0:
        candidates = [i for i in range(1, count) if counts[i] < largest] or [i for i in range(1, count) if counts[i] < limit]
        mass, budget = sum([portions[i] for i in candidates]), spare
        for i in candidates:
            more = min(limit - counts[i], max(1, budget * portions[i] // mass), spare)
            counts[i] = counts[i] + more
            spare = spare - more
    return np.array(counts)


def noise(key, extent, spread, most, pieces=(), kind=jnp.bfloat16):
    drawn = jax.random.normal(key, extent, jnp.float32) * spread
    if len(pieces) > 0:
        drawn = levels(key, extent, pieces, -0.22, 0.18) * drawn
    return jnp.clip(drawn, min=-most, max=most).astype(kind)


def setup_inputs(seed: int = 0) -> dict:
    key_list = jax.random.split(jax.random.key(seed), 10)
    handoff = noise(key_list[0], (SEGMENTS, ROWS, D), 1.0, 6.0, ((0, 2), (1, 16)))
    saved_inputs = noise(key_list[1], (SEGMENTS, ROWS, D), 1.0, 6.0, ((0, 2), (1, 16)))
    cotangent = noise(key_list[2], (SEGMENTS, ROWS, D), 1.0, 6.0, ((0, 2), (1, 16)))
    ids_forward_keys = jax.random.split(jax.random.fold_in(key_list[3], 1), SEGMENTS * ROWS // ROWS_DEV)
    ids_forward_turns = jax.random.permutation(jax.random.fold_in(key_list[3], 3), SEGMENTS * ROWS // ROWS_DEV)
    ids_forward = jax.vmap(lambda own, number: deal_out(jax.random.fold_in(key_list[3], 2), own, number, ROWS_DEV, ALL_EXPERTS, 2, CAP, 2))(ids_forward_keys, ids_forward_turns).reshape((SEGMENTS, ROWS, 2))
    gates_forward = jnp.clip(0.25 + 0.75 * jax.random.uniform(key_list[4], (SEGMENTS, ROWS, 2), jnp.float32) ** levels(key_list[4], (SEGMENTS, ROWS, 2), ((0, 2), (1, 16)), -0.2, 0.2), 0.25, 1.0)
    ids_backward_keys = jax.random.split(jax.random.fold_in(key_list[5], 1), SEGMENTS * ROWS // ROWS_DEV)
    ids_backward_turns = jax.random.permutation(jax.random.fold_in(key_list[5], 3), SEGMENTS * ROWS // ROWS_DEV)
    ids_backward = jax.vmap(lambda own, number: deal_out(jax.random.fold_in(key_list[5], 2), own, number, ROWS_DEV, ALL_EXPERTS, 2, CAP, 2))(ids_backward_keys, ids_backward_turns).reshape((SEGMENTS, ROWS, 2))
    gates_backward = jnp.clip(0.25 + 0.75 * jax.random.uniform(key_list[6], (SEGMENTS, ROWS, 2), jnp.float32) ** levels(key_list[6], (SEGMENTS, ROWS, 2), ((0, 2), (1, 16)), -0.2, 0.2), 0.25, 1.0)
    weight_in = noise(key_list[7], (SEGMENTS, D, EXPERTS * FF), D ** -0.5, 0.09375, ((0, 2), (2, 16)))
    weight_out = noise(key_list[8], (SEGMENTS, EXPERTS * FF, D), FF ** -0.5, 0.125, ((0, 2), (1, 16)))
    return dict(handoff=handoff, saved_inputs=saved_inputs, cotangent=cotangent, ids_forward=ids_forward, gates_forward=gates_forward, ids_backward=ids_backward, gates_backward=gates_backward, weight_in=weight_in, weight_out=weight_out)


def slot_tables(expert_ids, gate_values, experts):
    row_count = expert_ids.shape[0]
    flat_ids = expert_ids.reshape(row_count * 2).astype(jnp.int32)
    window = jnp.arange(experts, dtype=jnp.int32)
    member = (flat_ids[None, :] == window[:, None]).astype(jnp.int32)
    before = jnp.cumsum(member, axis=1, dtype=jnp.int32) - member
    positions = jnp.arange(CAP, dtype=jnp.int32)
    picked_slots = (member[:, None, :] * (before[:, None, :] == positions[None, :, None]).astype(jnp.int32)).astype(jnp.float32)
    picked_slots = picked_slots.reshape(experts * CAP, row_count, 2)
    select = jnp.sum(picked_slots, axis=2)
    weighted = jnp.sum(picked_slots * gate_values[None, :, :].astype(jnp.float32), axis=2)
    return select, weighted


def expert_rows(group_args):
    row_block, in_weight, out_weight = group_args
    preact = jnp.dot(row_block, in_weight, preferred_element_type=jnp.float32)
    hidden = jax.nn.silu(preact).astype(jnp.bfloat16)
    hidden_width = in_weight.shape[1] // GROUP
    terms = jnp.einsum("rgh,ghd->rgd", hidden.reshape(-1, GROUP, hidden_width).astype(jnp.float32),
                       out_weight.reshape(GROUP, hidden_width, -1).astype(jnp.float32))
    rounded = lax.optimization_barrier(terms.astype(jnp.bfloat16))
    return jnp.sum(rounded.astype(jnp.float32), axis=1)


def expert_grads(group_args):
    row_block, grad_block, in_weight, out_weight = group_args
    preact = jnp.dot(row_block, in_weight, preferred_element_type=jnp.float32)
    sigmoid_v = jax.nn.sigmoid(preact)
    slope_v = sigmoid_v * (1.0 + preact * (1.0 - sigmoid_v))
    grad_hidden = jnp.dot(grad_block, out_weight.T, preferred_element_type=jnp.float32)
    grad_pre = (grad_hidden * slope_v).astype(jnp.bfloat16)
    hidden_width = in_weight.shape[1] // GROUP
    terms = jnp.einsum("rgh,ghd->rgd", grad_pre.reshape(-1, GROUP, hidden_width).astype(jnp.float32),
                       in_weight.T.reshape(GROUP, hidden_width, -1).astype(jnp.float32))
    rounded = lax.optimization_barrier(terms.astype(jnp.bfloat16))
    return jnp.sum(rounded.astype(jnp.float32), axis=1)


def one_segment(segment_args):
    inputs, saved_block, upstream, ids_f, gates_f, ids_b, gates_b, in_weight, out_weight = segment_args
    experts = N_EXPERT // GROUP
    sources = inputs.shape[0] // ROWS_DEV
    feature_width = inputs.shape[1]
    tables = jax.vmap(partial(slot_tables, experts=experts))
    highest = lax.Precision.HIGHEST
    in_experts = in_weight.reshape(feature_width, experts, FF).transpose(1, 0, 2)
    out_experts = out_weight.reshape(experts, FF, feature_width)

    select_f, weigh_f = tables(ids_f.reshape(sources, ROWS_DEV, 2), gates_f.reshape(sources, ROWS_DEV, 2))
    picked = jnp.einsum("sqr,srd->sqd", select_f, inputs.reshape(sources, ROWS_DEV, feature_width).astype(jnp.float32),
                        precision=highest).astype(jnp.bfloat16)
    by_expert = picked.reshape(sources, experts, CAP, feature_width).transpose(1, 0, 2, 3).reshape(experts, sources * CAP, feature_width)
    outputs = lax.map(expert_rows, (by_expert, in_experts, out_experts))
    outputs = outputs.reshape(experts, sources, CAP, feature_width).transpose(1, 0, 2, 3).reshape(sources, experts * CAP, feature_width)
    mixed = jnp.einsum("sqr,sqd->srd", weigh_f, outputs, precision=highest).astype(jnp.bfloat16).reshape(-1, feature_width)

    select_b, weigh_b = tables(ids_b.reshape(sources, ROWS_DEV, 2), gates_b.reshape(sources, ROWS_DEV, 2))
    rows_back = jnp.einsum("sqr,srd->sqd", select_b, saved_block.reshape(sources, ROWS_DEV, feature_width).astype(jnp.float32),
                           precision=highest).astype(jnp.bfloat16)
    grads_out = jnp.einsum("sqr,srd->sqd", weigh_b, upstream.reshape(sources, ROWS_DEV, feature_width).astype(jnp.float32),
                           precision=highest).astype(jnp.bfloat16)
    rows_expert = rows_back.reshape(sources, experts, CAP, feature_width).transpose(1, 0, 2, 3).reshape(experts, sources * CAP, feature_width)
    grads_expert = grads_out.reshape(sources, experts, CAP, feature_width).transpose(1, 0, 2, 3).reshape(experts, sources * CAP, feature_width)
    slot_grads = lax.map(expert_grads, (rows_expert, grads_expert, in_experts, out_experts))
    slot_grads = slot_grads.reshape(experts, sources, CAP, feature_width).transpose(1, 0, 2, 3).reshape(sources, experts * CAP, feature_width)
    grads = jnp.einsum("sqr,sqd->srd", select_b, slot_grads, precision=highest).astype(jnp.bfloat16).reshape(-1, feature_width)
    return mixed, grads


def reference(handoff, saved_inputs, cotangent, ids_forward, gates_forward, ids_backward, gates_backward, weight_in, weight_out):
    inputs = jnp.concatenate([handoff[:1], handoff[:-1]], axis=0)
    upstream = jnp.concatenate([cotangent[1:], cotangent[-1:]], axis=0)
    expert_mix, input_grads = lax.map(one_segment, (inputs, saved_inputs, upstream, ids_forward, gates_forward,
                                                   ids_backward, gates_backward, weight_in, weight_out))
    return expert_mix, input_grads
```

```python
import functools

import jax
import jax.numpy as jnp
from jax import lax
from jax.experimental import pallas as pl
from jax.experimental.pallas import tpu as pltpu
from jax.sharding import PartitionSpec as P

GROUP = 16
CAP = 5


def shifted(block, axis, distance):
    devices = range(lax.axis_size(axis))
    route = [(i - distance, i) for i in devices if i - distance in devices]
    return lax.ppermute(block, axis, route)


def slot_tables(expert_ids, gate_values, experts):
    row_count = expert_ids.shape[0]
    flat_ids = expert_ids.reshape(row_count * 2)
    window = jnp.arange(experts, dtype=jnp.int32)
    member = (flat_ids[None, :] == window[:, None]).astype(jnp.int32)
    before = jnp.cumsum(member, axis=1, dtype=jnp.int32) - member
    positions = jnp.arange(CAP, dtype=jnp.int32)
    picked_slots = (
        member[:, None, :] * (before[:, None, :] == positions[None, :, None]).astype(jnp.int32)
    ).astype(jnp.float32)
    picked_slots = picked_slots.reshape(experts * CAP, row_count, 2)
    select = jnp.sum(picked_slots, axis=2)
    weighted = jnp.sum(picked_slots * gate_values[None, :, :], axis=2)
    return (select, weighted)


def pack_direct(stacked, groups):
    stacks = stacked.shape[0]
    feature_width = stacked.shape[2]
    shaped = stacked.reshape(stacks, groups, 1, CAP, feature_width)
    spread_out = jnp.broadcast_to(shaped, (stacks, groups, GROUP, CAP, feature_width))
    return spread_out.reshape(stacks, groups * GROUP, CAP, feature_width)


def expert_forward(arriving, local_in, local_out):
    feature_width = arriving.shape[-1]
    preact = jnp.dot(
        arriving.reshape(-1, feature_width), local_in, preferred_element_type=jnp.float32
    )
    hidden = jax.nn.silu(preact).astype(jnp.bfloat16)
    partial_out = jnp.dot(hidden, local_out, preferred_element_type=jnp.float32).astype(
        jnp.bfloat16
    )
    return partial_out.reshape(arriving.shape)


def expert_backward(row_part, grad_part, local_in, local_out):
    feature_width = row_part.shape[-1]
    preact = jnp.dot(
        row_part.reshape(-1, feature_width), local_in, preferred_element_type=jnp.float32
    )
    sigmoid_v = jax.nn.sigmoid(preact)
    slope_v = sigmoid_v * (1.0 + preact * (1.0 - sigmoid_v))
    grad_hidden = jnp.einsum(
        "rd,hd->rh",
        grad_part.reshape(-1, feature_width),
        local_out,
        preferred_element_type=jnp.float32,
    )
    grad_pre = (grad_hidden * slope_v).astype(jnp.bfloat16)
    partial_grad = jnp.einsum(
        "rh,dh->rd", grad_pre, local_in, preferred_element_type=jnp.float32
    ).astype(jnp.bfloat16)
    return partial_grad.reshape(row_part.shape)


def gather_groups(returned, groups):
    feature_width = returned.shape[-1]
    summed = jnp.sum(
        returned.reshape(groups, GROUP, CAP, feature_width).astype(jnp.float32), axis=1
    )
    return summed.reshape(groups * CAP, feature_width)


def per_device(
    handoff,
    saved_inputs,
    cotangent,
    ids_forward,
    gates_forward,
    ids_backward,
    gates_backward,
    weight_in,
    weight_out,
):
    highest = lax.Precision.HIGHEST
    groups = lax.axis_size("expert") // GROUP
    segment_index = lax.axis_index("segment")
    last_segment = lax.axis_size("segment") - 1
    arrived = shifted(handoff, "segment", 1)
    inputs = jnp.where(segment_index == 0, handoff, arrived)[0]
    returned = shifted(cotangent, "segment", -1)
    upstream = jnp.where(segment_index == last_segment, cotangent, returned)[0]
    local_in = weight_in[0]
    local_out = weight_out[0]
    select_f, weigh_f = slot_tables(ids_forward[0], gates_forward[0], groups)
    picked = jnp.dot(
        select_f.astype(jnp.bfloat16), inputs, preferred_element_type=jnp.float32
    ).astype(jnp.bfloat16)
    select_b, weigh_b = slot_tables(ids_backward[0], gates_backward[0], groups)
    rows_back = jnp.dot(
        select_b.astype(jnp.bfloat16), saved_inputs[0], preferred_element_type=jnp.float32
    ).astype(jnp.bfloat16)
    grads_out = jnp.dot(
        weigh_b, upstream.astype(jnp.float32), precision=highest, preferred_element_type=jnp.float32
    ).astype(jnp.bfloat16)
    backward_stack = jnp.stack([rows_back, grads_out])
    arriving_f = lax.all_to_all(
        pack_direct(picked[None], groups), "expert", split_axis=1, concat_axis=1, tiled=True
    )
    arriving_b = lax.all_to_all(
        pack_direct(backward_stack, groups), "expert", split_axis=1, concat_axis=1, tiled=True
    )
    partial_f = expert_forward(arriving_f[0], local_in, local_out)
    back_f = lax.all_to_all(partial_f, "expert", split_axis=0, concat_axis=0, tiled=True)
    combined = gather_groups(back_f, groups)
    expert_mix = jnp.dot(
        weigh_f.T, combined, precision=highest, preferred_element_type=jnp.float32
    ).astype(jnp.bfloat16)
    partial_b = expert_backward(arriving_b[0], arriving_b[1], local_in, local_out)
    back_b = lax.all_to_all(partial_b, "expert", split_axis=0, concat_axis=0, tiled=True)
    slot_grads = gather_groups(back_b, groups)
    input_grads = jnp.dot(
        select_b.T, slot_grads, precision=highest, preferred_element_type=jnp.float32
    ).astype(jnp.bfloat16)
    return (expert_mix[None], input_grads[None])


MESH = pl.DeviceIdType.MESH
BLOCK = 16
LANES = 128


def flipped(position, mask):
    bit = 1
    while bit <= mask:
        if mask & bit:
            position = position + bit * (1 - 2 * ((position // bit) % 2))
        bit *= 2
    return position


def exchange_kernel(
    planes,
    wire,
    ids_f,
    gates_f,
    ids_b,
    gates_b,
    handoff,
    saved,
    cotangent,
    weight_in,
    weight_out,
    out_f,
    out_b,
    rows_x,
    rows_s,
    w_in_side,
    w_out_side,
    blocks,
    req_send,
    req_recv,
    resp_send,
    resp_recv,
    own_rows,
    pair_send,
    pair_keep,
    pair_recv,
    y_send,
    y_keep,
    y_recv,
    z_send,
    z_recv,
    own_sum,
    local_sem,
    send_sem,
    recv_sem,
):
    segment = lax.axis_index("segment")
    expert = lax.axis_index("expert")
    row_count, width = rows_x.shape
    tail_width = width - wire
    hidden = weight_out.shape[0]

    def at_expert(mask):
        return {"expert": flipped(expert, mask)}

    other_segment = {"segment": 1 - segment}
    sibling = at_expert(1)
    across = at_expert(2)
    mates = [None] + [at_expert(4 * k) for k in range(1, planes)]

    barrier = pltpu.get_barrier_semaphore()
    partners = [other_segment, sibling, across] + mates[1:]
    for partner in partners:
        pl.semaphore_signal(barrier, inc=1, device_id=partner, device_id_type=MESH)

    @pl.when(segment == 0)
    def _():
        pltpu.make_async_copy(handoff, rows_x, local_sem.at[0]).start()

    @pl.when(segment != 0)
    def _():
        pltpu.make_async_copy(cotangent, rows_x, local_sem.at[0]).start()

    load_x = pltpu.make_async_copy(handoff, rows_x, local_sem.at[0])
    load_s = pltpu.make_async_copy(saved, rows_s, local_sem.at[1])
    load_in = pltpu.make_async_copy(weight_in, w_in_side.at[:, 0:hidden], local_sem.at[2])
    load_out = pltpu.make_async_copy(weight_out, w_out_side.at[0:hidden, :], local_sem.at[3])
    load_s.start()
    load_in.start()
    load_out.start()

    count = [0]
    started = []

    def remote(source, target, device):
        number = count[0]
        count[0] += 1
        return pltpu.make_async_remote_copy(
            src_ref=source,
            dst_ref=target,
            send_sem=send_sem.at[number],
            recv_sem=recv_sem.at[number],
            device_id=device,
            device_id_type=MESH,
        )

    def begin(copy):
        copy.start()
        started.append(copy)

    request = remote(req_send, req_recv, other_segment)
    response = remote(resp_send, resp_recv, other_segment)
    gather_z = [None] + [remote(blocks.at[0, 0, 0], blocks.at[k, 0, 0], mates[k]) for k in range(1, planes)]
    gather_y = [remote(blocks.at[k, 0, 0], blocks.at[k, 1, 0], across) for k in range(planes)]
    gather_c0 = [remote(blocks.at[k, 0, 0], blocks.at[k, 0, 1], sibling) for k in range(planes)]
    gather_c1 = [remote(blocks.at[k, 1, 0], blocks.at[k, 1, 1], sibling) for k in range(planes)]
    reduce_c = [remote(pair_send.at[k], pair_recv.at[k], sibling) for k in range(planes)]
    reduce_y = [remote(y_send.at[k], y_recv.at[k], across) for k in range(planes)]
    reduce_z = [None] + [remote(z_send.at[k], z_recv.at[k], mates[k]) for k in range(1, planes)]

    def ranks(ids, gates):
        first, second = ids[:, 0:1] == 0, ids[:, 1:2] == 0
        member = jnp.where(first | second, 1.0, 0.0)
        gate = jnp.where(first, gates[:, 0:1], 0.0) + jnp.where(second, gates[:, 1:2], 0.0)
        earlier = lax.broadcasted_iota(jnp.int32, (row_count, row_count), 1) < lax.broadcasted_iota(
            jnp.int32, (row_count, row_count), 0
        )
        wide = jnp.broadcast_to(member, (row_count, LANES))
        rank = jnp.dot(
            jnp.where(earlier, 1.0, 0.0).astype(jnp.bfloat16),
            wide.astype(jnp.bfloat16),
            preferred_element_type=jnp.float32,
        )
        return wide, rank.astype(jnp.int32), jnp.broadcast_to(gate, (row_count, LANES))

    lane = lax.broadcasted_iota(jnp.int32, (row_count, LANES), 1)

    def placed(member, rank, offset, at=lane):
        slot = at - offset
        fits = (slot == rank) & (slot < CAP) & (slot >= 0)
        return jnp.where(fits, member, 0.0)

    member_f, rank_f, gate_f = ranks(ids_f, gates_f)
    member_b, rank_b, gate_b = ranks(ids_b, gates_b)
    table = (
        placed(member_f, rank_f, 0)
        + placed(member_b, rank_b, CAP)
        + placed(member_b, rank_b, 2 * CAP) * gate_b
    )
    unit = jnp.where(
        lax.broadcasted_iota(jnp.int32, (BLOCK, LANES), 0)
        == lax.broadcasted_iota(jnp.int32, (BLOCK, LANES), 1),
        1.0,
        0.0,
    )
    by_slot = lax.dot_general(
        unit,
        table,
        (((1,), (1,)), ((), ())),
        precision=lax.Precision.HIGHEST,
        preferred_element_type=jnp.float32,
    )
    slot_row = lax.broadcasted_iota(jnp.int32, (BLOCK, row_count), 0)

    def rows_from(low):
        return jnp.where((slot_row >= low) & (slot_row < low + CAP), by_slot, 0.0)

    asked = rows_from((1 - segment) * (2 * CAP))
    mine = rows_from(segment * (2 * CAP))
    kept = rows_from(CAP)
    req_send[...] = jnp.concatenate([asked, jnp.zeros((BLOCK, LANES - row_count), jnp.float32)], axis=1)
    pl.semaphore_wait(barrier, len(partners))
    begin(request)

    def picked(weights, rows_ref):
        scale = jnp.sum(weights, axis=1, keepdims=True)
        choose = jnp.where(weights != 0.0, 1.0, 0.0).astype(jnp.bfloat16)
        return jnp.dot(choose, rows_ref[...], preferred_element_type=jnp.float32) * scale

    load_x.wait()
    load_s.wait()
    own_rows[...] = picked(mine, rows_x) + picked(kept, rows_s)
    request.wait_recv()
    resp_send[...] = picked(req_recv[:, 0:row_count], rows_x).astype(jnp.bfloat16)
    begin(response)
    load_in.wait()
    load_out.wait()
    turn = 512 if width % 512 == 0 else LANES

    def transposes(step, carry):
        piece = pl.ds(pl.multiple_of(step * turn, turn), turn)
        w_in_side[piece, hidden : 2 * hidden] = w_out_side[0:hidden, piece].T
        w_out_side[hidden : 2 * hidden, piece] = w_in_side[piece, 0:hidden].T
        return carry

    lax.fori_loop(0, width // turn, transposes, 0)
    response.wait_recv()
    blocks[0, 0, 0] = (own_rows[...] + resp_recv[...].astype(jnp.float32)).astype(jnp.bfloat16)

    def spread(k):
        if k > 0:
            gather_z[k].wait_recv()
        begin(gather_y[k])
        begin(gather_c0[k])

    def relay(k):
        gather_y[k].wait_recv()
        begin(gather_c1[k])

    batch = 4 * BLOCK
    place = lax.broadcasted_iota(jnp.int32, (batch, hidden), 0) % BLOCK
    chunk = 256 if tail_width % 256 == 0 and wire % 256 == 0 else LANES

    def compute(k):
        gather_c0[k].wait_recv()
        gather_c1[k].wait_recv()

        def contract(step, total):
            piece = pl.ds(pl.multiple_of(step * turn, turn), turn)
            return total + jnp.dot(
                blocks[k, :, :, :, piece].reshape(batch, turn),
                w_in_side[piece, :],
                preferred_element_type=jnp.float32,
            )

        both = lax.fori_loop(
            0, width // turn, contract, jnp.zeros((batch, 2 * hidden), jnp.float32), unroll=True
        )
        pre = both[:, 0:hidden]
        grad_hidden = pltpu.roll(both[:, hidden:], batch - CAP, 0)
        gate = 1.0 / (1.0 + jnp.exp(-pre))
        forward = jnp.where(place < CAP, pre * gate, 0.0)
        slope = gate * (1.0 + pre * (1.0 - gate))
        backward = jnp.where((place >= CAP) & (place < 2 * CAP), grad_hidden * slope, 0.0)
        late_f = pltpu.roll(forward, 2 * CAP, 0).astype(jnp.bfloat16)
        late_b = pltpu.roll(backward, CAP, 0).astype(jnp.bfloat16)
        main = jnp.concatenate([forward, backward], axis=1).astype(jnp.bfloat16)

        def put(start, value):
            columns = pl.ds(start, chunk)
            value = value.reshape(2, 2, BLOCK, chunk)
            pair_keep[k, :, :, columns] = value[:, 0]
            pair_send[k, :, :, columns] = value[:, 1].astype(jnp.bfloat16)

        def product(start):
            return jnp.dot(main, w_out_side[:, pl.ds(start, chunk)], preferred_element_type=jnp.float32)

        def pieces(step, carry):
            start = pl.multiple_of(step * chunk, chunk)
            late = pl.ds(pl.multiple_of(wire + step * chunk, chunk), chunk)
            put(
                start,
                product(start)
                + jnp.dot(late_f, w_out_side[0:hidden, late], preferred_element_type=jnp.float32),
            )
            start = pl.multiple_of(tail_width + step * chunk, chunk)
            put(
                start,
                product(start)
                + jnp.dot(
                    late_b, w_out_side[hidden : 2 * hidden, late], preferred_element_type=jnp.float32
                ),
            )
            return carry

        lax.fori_loop(0, tail_width // chunk, pieces, 0, unroll=True)
        for start in range(2 * tail_width, wire, chunk):
            put(start, product(start))
        begin(reduce_c[k])

    def join_pair(k):
        reduce_c[k].wait_recv()
        y_send[k] = (pair_keep[k, 1] + pair_recv[k, 1].astype(jnp.float32)).astype(jnp.bfloat16)
        begin(reduce_y[k])
        y_keep[k] = pair_keep[k, 0] + pair_recv[k, 0].astype(jnp.float32)

    def join_plane(k):
        reduce_y[k].wait_recv()
        total = y_keep[k] + y_recv[k].astype(jnp.float32)
        if k == 0:
            own_sum[...] = total
        else:
            z_send[k] = total.astype(jnp.bfloat16)
            begin(reduce_z[k])

    for k in range(1, planes):
        begin(gather_z[k])
    spread(0)
    for step in range(planes + 2):
        if step + 1 < planes:
            spread(step + 1)
        if step < planes:
            relay(step)
        if 0 <= step - 1 < planes:
            join_pair(step - 1)
        if 0 <= step - 2 < planes:
            join_plane(step - 2)
        if step < planes:
            compute(step)

    lane_half = lane % BLOCK

    def spread_out(member, rank, offset):
        ones = placed(member, rank, offset, lane_half)
        return jnp.where(lane < 2 * BLOCK, ones, 0.0)[:, 0 : 2 * BLOCK].astype(jnp.bfloat16)

    heads = jnp.concatenate([spread_out(member_f, rank_f, 0), spread_out(member_b, rank_b, CAP)], axis=0)
    late_rows_f = spread_out(member_f, rank_f, 2 * CAP)
    late_rows_b = spread_out(member_b, rank_b, 2 * CAP)
    gate_wide = jnp.concatenate([gate_f] * (chunk // LANES), axis=1)
    for k in range(1, planes):
        reduce_z[k].wait_recv()

    def halves(start):
        columns = slice(start, start + chunk)
        total = own_sum[:, columns]
        for k in range(1, planes):
            total = total + z_recv[k, :, columns].astype(jnp.float32)
        high = total.astype(jnp.bfloat16)
        low = (total - high.astype(jnp.float32)).astype(jnp.bfloat16)
        return jnp.concatenate([high, low], axis=0)

    for start in range(0, wire, chunk):
        both = halves(start)
        value = jnp.dot(heads, both, preferred_element_type=jnp.float32)
        out_f[:, start : start + chunk] = (value[0:row_count] * gate_wide).astype(jnp.bfloat16)
        out_b[:, start : start + chunk] = value[row_count:].astype(jnp.bfloat16)
        if start < tail_width:
            value = jnp.dot(late_rows_f, both, preferred_element_type=jnp.float32) * gate_wide
            out_f[:, wire + start : wire + start + chunk] = value.astype(jnp.bfloat16)
        elif start < 2 * tail_width:
            late = wire + start - tail_width
            value = jnp.dot(late_rows_b, both, preferred_element_type=jnp.float32)
            out_b[:, late : late + chunk] = value.astype(jnp.bfloat16)
    for copy in started:
        copy.wait_send()


def exchange(planes, handoff, saved_inputs, cotangent, ids_forward, gates_forward, ids_backward, gates_backward, weight_in, weight_out):
    rows, width = handoff.shape[1:]
    hidden = weight_out.shape[1]
    tiles = width // LANES
    wire = -(-2 * tiles // 3) * LANES
    bf16, f32 = jnp.bfloat16, jnp.float32
    copies = 2 + 2 * (planes - 1) + 5 * planes
    vmem = pl.BlockSpec(memory_space=pltpu.VMEM)
    hbm = pl.BlockSpec(memory_space=pl.ANY)
    mixed, grads = pl.pallas_call(
        functools.partial(exchange_kernel, planes, wire),
        out_shape=[jax.ShapeDtypeStruct((rows, width), bf16)] * 2,
        in_specs=[vmem] * 4 + [hbm] * 5,
        out_specs=[vmem] * 2,
        scratch_shapes=[
            pltpu.VMEM((rows, width), bf16),
            pltpu.VMEM((rows, width), bf16),
            pltpu.VMEM((width, 2 * hidden), bf16),
            pltpu.VMEM((2 * hidden, width), bf16),
            pltpu.VMEM((planes, 2, 2, BLOCK, width), bf16),
            pltpu.VMEM((BLOCK, LANES), f32),
            pltpu.VMEM((BLOCK, LANES), f32),
            pltpu.VMEM((BLOCK, width), bf16),
            pltpu.VMEM((BLOCK, width), bf16),
            pltpu.VMEM((BLOCK, width), f32),
            pltpu.VMEM((planes, 2, BLOCK, wire), bf16),
            pltpu.VMEM((planes, 2, BLOCK, wire), f32),
            pltpu.VMEM((planes, 2, BLOCK, wire), bf16),
            pltpu.VMEM((planes, BLOCK, wire), bf16),
            pltpu.VMEM((planes, BLOCK, wire), f32),
            pltpu.VMEM((planes, BLOCK, wire), bf16),
            pltpu.VMEM((planes, BLOCK, wire), bf16),
            pltpu.VMEM((planes, BLOCK, wire), bf16),
            pltpu.VMEM((BLOCK, wire), f32),
            pltpu.SemaphoreType.DMA((4,)),
            pltpu.SemaphoreType.DMA((copies,)),
            pltpu.SemaphoreType.DMA((copies,)),
        ],
        compiler_params=pltpu.CompilerParams(
            collective_id=0, has_side_effects=True, vmem_limit_bytes=48 * 1024 * 1024
        ),
    )(
        ids_forward[0],
        gates_forward[0],
        ids_backward[0],
        gates_backward[0],
        handoff[0],
        saved_inputs[0],
        cotangent[0],
        weight_in[0],
        weight_out[0],
    )
    return (mixed[None], grads[None])


def device_body(mesh):
    segments, experts = mesh.shape["segment"], mesh.shape["expert"]
    planes = experts // 4
    if segments == 2 and experts == GROUP and planes & (planes - 1) == 0:
        return functools.partial(exchange, planes)
    return per_device


def solution(mesh):
    return jax.shard_map(
        device_body(mesh),
        mesh=mesh,
        in_specs=(
            P("segment", "expert", None),
            P("segment", "expert", None),
            P("segment", "expert", None),
            P("segment", "expert", None),
            P("segment", "expert", None),
            P("segment", "expert", None),
            P("segment", "expert", None),
            P("segment", None, "expert"),
            P("segment", "expert", None),
        ),
        out_specs=(P("segment", "expert", None), P("segment", "expert", None)),
        check_vma=False,
    )
```

```python
import functools

import jax
import jax.numpy as jnp
from jax import lax
from jax.experimental import pallas as pl
from jax.experimental.pallas import tpu as pltpu
from jax.sharding import PartitionSpec as P

GROUP = 16
CAP = 5


def shifted(block, axis, distance):
    devices = range(lax.axis_size(axis))
    route = [(i - distance, i) for i in devices if i - distance in devices]
    return lax.ppermute(block, axis, route)


def slot_tables(expert_ids, gate_values, experts):
    row_count = expert_ids.shape[0]
    flat_ids = expert_ids.reshape(row_count * 2)
    window = jnp.arange(experts, dtype=jnp.int32)
    member = (flat_ids[None, :] == window[:, None]).astype(jnp.int32)
    before = jnp.cumsum(member, axis=1, dtype=jnp.int32) - member
    positions = jnp.arange(CAP, dtype=jnp.int32)
    picked_slots = (
        member[:, None, :] * (before[:, None, :] == positions[None, :, None]).astype(jnp.int32)
    ).astype(jnp.float32)
    picked_slots = picked_slots.reshape(experts * CAP, row_count, 2)
    select = jnp.sum(picked_slots, axis=2)
    weighted = jnp.sum(picked_slots * gate_values[None, :, :], axis=2)
    return (select, weighted)


def pack_direct(stacked, groups):
    stacks = stacked.shape[0]
    feature_width = stacked.shape[2]
    shaped = stacked.reshape(stacks, groups, 1, CAP, feature_width)
    spread_out = jnp.broadcast_to(shaped, (stacks, groups, GROUP, CAP, feature_width))
    return spread_out.reshape(stacks, groups * GROUP, CAP, feature_width)


def expert_forward(arriving, local_in, local_out):
    feature_width = arriving.shape[-1]
    preact = jnp.dot(
        arriving.reshape(-1, feature_width), local_in, preferred_element_type=jnp.float32
    )
    hidden = jax.nn.silu(preact).astype(jnp.bfloat16)
    partial_out = jnp.dot(hidden, local_out, preferred_element_type=jnp.float32).astype(
        jnp.bfloat16
    )
    return partial_out.reshape(arriving.shape)


def expert_backward(row_part, grad_part, local_in, local_out):
    feature_width = row_part.shape[-1]
    preact = jnp.dot(
        row_part.reshape(-1, feature_width), local_in, preferred_element_type=jnp.float32
    )
    sigmoid_v = jax.nn.sigmoid(preact)
    slope_v = sigmoid_v * (1.0 + preact * (1.0 - sigmoid_v))
    grad_hidden = jnp.einsum(
        "rd,hd->rh",
        grad_part.reshape(-1, feature_width),
        local_out,
        preferred_element_type=jnp.float32,
    )
    grad_pre = (grad_hidden * slope_v).astype(jnp.bfloat16)
    partial_grad = jnp.einsum(
        "rh,dh->rd", grad_pre, local_in, preferred_element_type=jnp.float32
    ).astype(jnp.bfloat16)
    return partial_grad.reshape(row_part.shape)


def gather_groups(returned, groups):
    feature_width = returned.shape[-1]
    summed = jnp.sum(
        returned.reshape(groups, GROUP, CAP, feature_width).astype(jnp.float32), axis=1
    )
    return summed.reshape(groups * CAP, feature_width)


def per_device(
    handoff,
    saved_inputs,
    cotangent,
    ids_forward,
    gates_forward,
    ids_backward,
    gates_backward,
    weight_in,
    weight_out,
):
    highest = lax.Precision.HIGHEST
    groups = lax.axis_size("expert") // GROUP
    segment_index = lax.axis_index("segment")
    last_segment = lax.axis_size("segment") - 1
    arrived = shifted(handoff, "segment", 1)
    inputs = jnp.where(segment_index == 0, handoff, arrived)[0]
    returned = shifted(cotangent, "segment", -1)
    upstream = jnp.where(segment_index == last_segment, cotangent, returned)[0]
    local_in = weight_in[0]
    local_out = weight_out[0]
    select_f, weigh_f = slot_tables(ids_forward[0], gates_forward[0], groups)
    picked = jnp.dot(
        select_f.astype(jnp.bfloat16), inputs, preferred_element_type=jnp.float32
    ).astype(jnp.bfloat16)
    select_b, weigh_b = slot_tables(ids_backward[0], gates_backward[0], groups)
    rows_back = jnp.dot(
        select_b.astype(jnp.bfloat16), saved_inputs[0], preferred_element_type=jnp.float32
    ).astype(jnp.bfloat16)
    grads_out = jnp.dot(
        weigh_b, upstream.astype(jnp.float32), precision=highest, preferred_element_type=jnp.float32
    ).astype(jnp.bfloat16)
    backward_stack = jnp.stack([rows_back, grads_out])
    arriving_f = lax.all_to_all(
        pack_direct(picked[None], groups), "expert", split_axis=1, concat_axis=1, tiled=True
    )
    arriving_b = lax.all_to_all(
        pack_direct(backward_stack, groups), "expert", split_axis=1, concat_axis=1, tiled=True
    )
    partial_f = expert_forward(arriving_f[0], local_in, local_out)
    back_f = lax.all_to_all(partial_f, "expert", split_axis=0, concat_axis=0, tiled=True)
    combined = gather_groups(back_f, groups)
    expert_mix = jnp.dot(
        weigh_f.T, combined, precision=highest, preferred_element_type=jnp.float32
    ).astype(jnp.bfloat16)
    partial_b = expert_backward(arriving_b[0], arriving_b[1], local_in, local_out)
    back_b = lax.all_to_all(partial_b, "expert", split_axis=0, concat_axis=0, tiled=True)
    slot_grads = gather_groups(back_b, groups)
    input_grads = jnp.dot(
        select_b.T, slot_grads, precision=highest, preferred_element_type=jnp.float32
    ).astype(jnp.bfloat16)
    return (expert_mix[None], input_grads[None])


MESH = pl.DeviceIdType.MESH
BLOCK = 16
LANES = 128


def flipped(position, mask):
    bit = 1
    while bit <= mask:
        if mask & bit:
            position = position + bit * (1 - 2 * ((position // bit) % 2))
        bit *= 2
    return position


def exchange_kernel(
    planes,
    wire,
    ids_f_hbm,
    gates_f_hbm,
    ids_b_hbm,
    gates_b_hbm,
    handoff,
    saved,
    cotangent,
    weight_in,
    weight_out,
    out_f,
    out_b,
    rows_x,
    rows_s,
    w_in_side,
    w_out_side,
    blocks,
    req_send,
    req_recv,
    resp_send,
    resp_recv,
    own_rows,
    pair_send,
    pair_keep,
    pair_recv,
    y_send,
    y_keep,
    y_recv,
    z_send,
    z_recv,
    own_sum,
    ids_f,
    gates_f,
    ids_b,
    gates_b,
    scatter,
    gate_wide,
    local_sem,
    send_sem,
    recv_sem,
):
    segment = lax.axis_index("segment")
    expert = lax.axis_index("expert")
    row_count, width = rows_x.shape
    tail_width = width - wire
    hidden = weight_out.shape[0]

    def at_expert(mask):
        return {"expert": flipped(expert, mask)}

    other_segment = {"segment": 1 - segment}
    sibling = at_expert(1)
    across = at_expert(2)
    mates = [None] + [at_expert(4 * k) for k in range(1, planes)]

    barrier = pltpu.get_barrier_semaphore()
    partners = [other_segment, sibling, across] + mates[1:]
    for partner in partners:
        pl.semaphore_signal(barrier, inc=1, device_id=partner, device_id_type=MESH)

    tables = [
        pltpu.make_async_copy(source, target, local_sem.at[4 + i])
        for i, (source, target) in enumerate(
            [(ids_f_hbm, ids_f), (gates_f_hbm, gates_f), (ids_b_hbm, ids_b), (gates_b_hbm, gates_b)]
        )
    ]
    for table_copy in tables:
        table_copy.start()

    @pl.when(segment == 0)
    def _():
        pltpu.make_async_copy(handoff, rows_x, local_sem.at[0]).start()

    @pl.when(segment != 0)
    def _():
        pltpu.make_async_copy(cotangent, rows_x, local_sem.at[0]).start()

    load_x = pltpu.make_async_copy(handoff, rows_x, local_sem.at[0])
    load_s = pltpu.make_async_copy(saved, rows_s, local_sem.at[1])
    load_in = pltpu.make_async_copy(weight_in, w_in_side.at[:, 0:hidden], local_sem.at[2])
    load_out = pltpu.make_async_copy(weight_out, w_out_side.at[0:hidden, :], local_sem.at[3])
    load_s.start()
    load_in.start()
    load_out.start()

    count = [0]
    started = []

    def remote(source, target, device):
        number = count[0]
        count[0] += 1
        return pltpu.make_async_remote_copy(
            src_ref=source,
            dst_ref=target,
            send_sem=send_sem.at[number],
            recv_sem=recv_sem.at[number],
            device_id=device,
            device_id_type=MESH,
        )

    def begin(copy):
        copy.start()
        started.append(copy)

    request = remote(req_send, req_recv, other_segment)
    response = remote(resp_send, resp_recv, other_segment)
    gather_z = [None] + [remote(blocks.at[0, 0, 0], blocks.at[k, 0, 0], mates[k]) for k in range(1, planes)]
    gather_y = [remote(blocks.at[k, 0, 0], blocks.at[k, 1, 0], across) for k in range(planes)]
    gather_c0 = [remote(blocks.at[k, 0, 0], blocks.at[k, 0, 1], sibling) for k in range(planes)]
    gather_c1 = [remote(blocks.at[k, 1, 0], blocks.at[k, 1, 1], sibling) for k in range(planes)]
    reduce_c = [remote(pair_send.at[k], pair_recv.at[k], sibling) for k in range(planes)]
    reduce_y = [remote(y_send.at[k], y_recv.at[k], across) for k in range(planes)]
    reduce_z = [None] + [remote(z_send.at[k], z_recv.at[k], mates[k]) for k in range(1, planes)]

    for table_copy in tables:
        table_copy.wait()
    earlier = jnp.where(
        lax.broadcasted_iota(jnp.int32, (row_count, row_count), 0)
        < lax.broadcasted_iota(jnp.int32, (row_count, row_count), 1),
        1.0,
        0.0,
    ).astype(jnp.bfloat16)

    def ranks(ids, gates):
        first, second = ids[0:1, :] == 0, ids[1:2, :] == 0
        member = jnp.where(first | second, 1.0, 0.0)
        gate = jnp.where(first, gates[0:1, :], 0.0) + jnp.where(second, gates[1:2, :], 0.0)
        wide = jnp.broadcast_to(member, (BLOCK, row_count))
        rank = jnp.dot(wide.astype(jnp.bfloat16), earlier, preferred_element_type=jnp.float32)
        return wide, rank.astype(jnp.int32), gate

    slot_row = lax.broadcasted_iota(jnp.int32, (BLOCK, row_count), 0)

    def placed(member, rank, offset):
        slot = slot_row - offset
        fits = (slot == rank) & (slot < CAP) & (slot >= 0)
        return jnp.where(fits, member, 0.0)

    member_f, rank_f, gate_f = ranks(ids_f, gates_f)
    member_b, rank_b, gate_b = ranks(ids_b, gates_b)
    by_slot = (
        placed(member_f, rank_f, 0)
        + placed(member_b, rank_b, CAP)
        + placed(member_b, rank_b, 2 * CAP) * gate_b
    )

    def rows_from(low):
        return jnp.where((slot_row >= low) & (slot_row < low + CAP), by_slot, 0.0)

    asked = rows_from((1 - segment) * (2 * CAP))
    mine = rows_from(segment * (2 * CAP))
    kept = rows_from(CAP)
    req_send[...] = jnp.concatenate([asked, jnp.zeros((BLOCK, LANES - row_count), jnp.float32)], axis=1)
    pl.semaphore_wait(barrier, len(partners))
    begin(request)

    def picked(weights, rows_ref):
        scale = jnp.sum(weights, axis=1, keepdims=True)
        choose = jnp.where(weights != 0.0, 1.0, 0.0).astype(jnp.bfloat16)
        return jnp.dot(choose, rows_ref[...], preferred_element_type=jnp.float32) * scale

    load_x.wait()
    load_s.wait()
    own_rows[...] = picked(mine, rows_x) + picked(kept, rows_s)
    request.wait_recv()
    resp_send[...] = picked(req_recv[:, 0:row_count], rows_x).astype(jnp.bfloat16)
    begin(response)
    load_in.wait()
    load_out.wait()
    turn = 512 if width % 512 == 0 else LANES

    def transposes(step, carry):
        piece = pl.ds(pl.multiple_of(step * turn, turn), turn)
        w_in_side[piece, hidden : 2 * hidden] = w_out_side[0:hidden, piece].T
        w_out_side[hidden : 2 * hidden, piece] = w_in_side[piece, 0:hidden].T
        return carry

    lax.fori_loop(0, width // turn, transposes, 0)
    unit = jnp.where(
        lax.broadcasted_iota(jnp.int32, (row_count, row_count), 0)
        == lax.broadcasted_iota(jnp.int32, (row_count, row_count), 1),
        1.0,
        0.0,
    )
    by_row = (((1,), (1,)), ((), ()))
    for i, (member, rank, offset) in enumerate(
        [(member_f, rank_f, 0), (member_b, rank_b, CAP), (member_f, rank_f, 2 * CAP), (member_b, rank_b, 2 * CAP)]
    ):
        ones = placed(member, rank, offset)
        scatter[i] = lax.dot_general(
            unit.astype(jnp.bfloat16),
            jnp.concatenate([ones, ones], axis=0).astype(jnp.bfloat16),
            by_row,
            preferred_element_type=jnp.float32,
        ).astype(jnp.bfloat16)
    gate_wide[...] = lax.dot_general(
        unit,
        jnp.broadcast_to(gate_f, (LANES, row_count)),
        by_row,
        precision=lax.Precision.HIGHEST,
        preferred_element_type=jnp.float32,
    )
    response.wait_recv()
    blocks[0, 0, 0] = (own_rows[...] + resp_recv[...].astype(jnp.float32)).astype(jnp.bfloat16)

    def spread(k):
        if k > 0:
            gather_z[k].wait_recv()
        begin(gather_y[k])
        begin(gather_c0[k])

    def relay(k):
        gather_y[k].wait_recv()
        begin(gather_c1[k])

    batch = 4 * BLOCK
    place = lax.broadcasted_iota(jnp.int32, (batch, hidden), 0) % BLOCK
    chunk = 256 if tail_width % 256 == 0 and wire % 256 == 0 else LANES

    def compute(k):
        gather_c0[k].wait_recv()
        gather_c1[k].wait_recv()

        def contract(step, total):
            piece = pl.ds(pl.multiple_of(step * turn, turn), turn)
            return total + jnp.dot(
                blocks[k, :, :, :, piece].reshape(batch, turn),
                w_in_side[piece, :],
                preferred_element_type=jnp.float32,
            )

        both = lax.fori_loop(
            0, width // turn, contract, jnp.zeros((batch, 2 * hidden), jnp.float32), unroll=True
        )
        pre = both[:, 0:hidden]
        grad_hidden = pltpu.roll(both[:, hidden:], batch - CAP, 0)
        gate = 1.0 / (1.0 + jnp.exp(-pre))
        forward = jnp.where(place < CAP, pre * gate, 0.0)
        slope = gate * (1.0 + pre * (1.0 - gate))
        backward = jnp.where((place >= CAP) & (place < 2 * CAP), grad_hidden * slope, 0.0)
        late_f = pltpu.roll(forward, 2 * CAP, 0).astype(jnp.bfloat16)
        late_b = pltpu.roll(backward, CAP, 0).astype(jnp.bfloat16)
        main = jnp.concatenate([forward, backward], axis=1).astype(jnp.bfloat16)

        def put(start, value):
            columns = pl.ds(start, chunk)
            value = value.reshape(2, 2, BLOCK, chunk)
            pair_keep[k, :, :, columns] = value[:, 0]
            pair_send[k, :, :, columns] = value[:, 1].astype(jnp.bfloat16)

        def product(start):
            return jnp.dot(main, w_out_side[:, pl.ds(start, chunk)], preferred_element_type=jnp.float32)

        def pieces(step, carry):
            start = pl.multiple_of(step * chunk, chunk)
            late = pl.ds(pl.multiple_of(wire + step * chunk, chunk), chunk)
            put(
                start,
                product(start)
                + jnp.dot(late_f, w_out_side[0:hidden, late], preferred_element_type=jnp.float32),
            )
            start = pl.multiple_of(tail_width + step * chunk, chunk)
            put(
                start,
                product(start)
                + jnp.dot(
                    late_b, w_out_side[hidden : 2 * hidden, late], preferred_element_type=jnp.float32
                ),
            )
            return carry

        lax.fori_loop(0, tail_width // chunk, pieces, 0, unroll=True)
        for start in range(2 * tail_width, wire, chunk):
            put(start, product(start))
        begin(reduce_c[k])

    def join_pair(k):
        reduce_c[k].wait_recv()
        y_send[k] = (pair_keep[k, 1] + pair_recv[k, 1].astype(jnp.float32)).astype(jnp.bfloat16)
        begin(reduce_y[k])
        y_keep[k] = pair_keep[k, 0] + pair_recv[k, 0].astype(jnp.float32)

    def join_plane(k):
        reduce_y[k].wait_recv()
        total = y_keep[k] + y_recv[k].astype(jnp.float32)
        if k == 0:
            own_sum[...] = total
        else:
            z_send[k] = total.astype(jnp.bfloat16)
            begin(reduce_z[k])

    for k in range(1, planes):
        begin(gather_z[k])
    spread(0)
    for step in range(planes + 2):
        if step + 1 < planes:
            spread(step + 1)
        if step < planes:
            relay(step)
        if 0 <= step - 1 < planes:
            join_pair(step - 1)
        if 0 <= step - 2 < planes:
            join_plane(step - 2)
        if step < planes:
            compute(step)

    heads = scatter[0:2].reshape(2 * row_count, 2 * BLOCK)
    late_rows_f, late_rows_b = scatter[2], scatter[3]
    wide_gate = jnp.concatenate([gate_wide[...]] * (chunk // LANES), axis=1)
    for k in range(1, planes):
        reduce_z[k].wait_recv()

    def halves(start):
        columns = slice(start, start + chunk)
        total = own_sum[:, columns]
        for k in range(1, planes):
            total = total + z_recv[k, :, columns].astype(jnp.float32)
        high = total.astype(jnp.bfloat16)
        low = (total - high.astype(jnp.float32)).astype(jnp.bfloat16)
        return jnp.concatenate([high, low], axis=0)

    for start in range(0, wire, chunk):
        both = halves(start)
        value = jnp.dot(heads, both, preferred_element_type=jnp.float32)
        out_f[:, start : start + chunk] = (value[0:row_count] * wide_gate).astype(jnp.bfloat16)
        out_b[:, start : start + chunk] = value[row_count:].astype(jnp.bfloat16)
        if start < tail_width:
            value = jnp.dot(late_rows_f, both, preferred_element_type=jnp.float32) * wide_gate
            out_f[:, wire + start : wire + start + chunk] = value.astype(jnp.bfloat16)
        elif start < 2 * tail_width:
            late = wire + start - tail_width
            value = jnp.dot(late_rows_b, both, preferred_element_type=jnp.float32)
            out_b[:, late : late + chunk] = value.astype(jnp.bfloat16)
    for copy in started:
        copy.wait_send()


def exchange(planes, handoff, saved_inputs, cotangent, ids_forward, gates_forward, ids_backward, gates_backward, weight_in, weight_out):
    rows, width = handoff.shape[1:]
    hidden = weight_out.shape[1]
    tiles = width // LANES
    wire = -(-2 * tiles // 3) * LANES
    bf16, f32 = jnp.bfloat16, jnp.float32
    copies = 2 + 2 * (planes - 1) + 5 * planes
    vmem = pl.BlockSpec(memory_space=pltpu.VMEM)
    hbm = pl.BlockSpec(memory_space=pl.ANY)
    mixed, grads = pl.pallas_call(
        functools.partial(exchange_kernel, planes, wire),
        out_shape=[jax.ShapeDtypeStruct((rows, width), bf16)] * 2,
        in_specs=[hbm] * 9,
        out_specs=[vmem] * 2,
        scratch_shapes=[
            pltpu.VMEM((rows, width), bf16),
            pltpu.VMEM((rows, width), bf16),
            pltpu.VMEM((width, 2 * hidden), bf16),
            pltpu.VMEM((2 * hidden, width), bf16),
            pltpu.VMEM((planes, 2, 2, BLOCK, width), bf16),
            pltpu.VMEM((BLOCK, LANES), f32),
            pltpu.VMEM((BLOCK, LANES), f32),
            pltpu.VMEM((BLOCK, width), bf16),
            pltpu.VMEM((BLOCK, width), bf16),
            pltpu.VMEM((BLOCK, width), f32),
            pltpu.VMEM((planes, 2, BLOCK, wire), bf16),
            pltpu.VMEM((planes, 2, BLOCK, wire), f32),
            pltpu.VMEM((planes, 2, BLOCK, wire), bf16),
            pltpu.VMEM((planes, BLOCK, wire), bf16),
            pltpu.VMEM((planes, BLOCK, wire), f32),
            pltpu.VMEM((planes, BLOCK, wire), bf16),
            pltpu.VMEM((planes, BLOCK, wire), bf16),
            pltpu.VMEM((planes, BLOCK, wire), bf16),
            pltpu.VMEM((BLOCK, wire), f32),
            pltpu.VMEM((2, rows), jnp.int32),
            pltpu.VMEM((2, rows), f32),
            pltpu.VMEM((2, rows), jnp.int32),
            pltpu.VMEM((2, rows), f32),
            pltpu.VMEM((4, rows, 2 * BLOCK), bf16),
            pltpu.VMEM((rows, LANES), f32),
            pltpu.SemaphoreType.DMA((8,)),
            pltpu.SemaphoreType.DMA((copies,)),
            pltpu.SemaphoreType.DMA((copies,)),
        ],
        compiler_params=pltpu.CompilerParams(
            collective_id=0, has_side_effects=True
        ),
    )(
        ids_forward[0].T,
        gates_forward[0].T,
        ids_backward[0].T,
        gates_backward[0].T,
        handoff[0],
        saved_inputs[0],
        cotangent[0],
        weight_in[0],
        weight_out[0],
    )
    return (mixed[None], grads[None])


def device_body(mesh):
    segments, experts = mesh.shape["segment"], mesh.shape["expert"]
    planes = experts // 4
    if segments == 2 and experts == GROUP and planes & (planes - 1) == 0:
        return functools.partial(exchange, planes)
    return per_device


def solution(mesh):
    return jax.shard_map(
        device_body(mesh),
        mesh=mesh,
        in_specs=(
            P("segment", "expert", None),
            P("segment", "expert", None),
            P("segment", "expert", None),
            P("segment", "expert", None),
            P("segment", "expert", None),
            P("segment", "expert", None),
            P("segment", "expert", None),
            P("segment", None, "expert"),
            P("segment", "expert", None),
        ),
        out_specs=(P("segment", "expert", None), P("segment", "expert", None)),
        check_vma=False,
    )
```

```python
import functools

import jax
import jax.numpy as jnp
from jax import lax
from jax.experimental import pallas as pl
from jax.experimental.pallas import tpu as pltpu
from jax.sharding import PartitionSpec as P

GROUP = 16
CAP = 5


def shifted(block, axis, distance):
    devices = range(lax.axis_size(axis))
    route = [(i - distance, i) for i in devices if i - distance in devices]
    return lax.ppermute(block, axis, route)


def slot_tables(expert_ids, gate_values, experts):
    row_count = expert_ids.shape[0]
    flat_ids = expert_ids.reshape(row_count * 2)
    window = jnp.arange(experts, dtype=jnp.int32)
    member = (flat_ids[None, :] == window[:, None]).astype(jnp.int32)
    before = jnp.cumsum(member, axis=1, dtype=jnp.int32) - member
    positions = jnp.arange(CAP, dtype=jnp.int32)
    picked_slots = (
        member[:, None, :] * (before[:, None, :] == positions[None, :, None]).astype(jnp.int32)
    ).astype(jnp.float32)
    picked_slots = picked_slots.reshape(experts * CAP, row_count, 2)
    select = jnp.sum(picked_slots, axis=2)
    weighted = jnp.sum(picked_slots * gate_values[None, :, :], axis=2)
    return (select, weighted)


def pack_direct(stacked, groups):
    stacks = stacked.shape[0]
    feature_width = stacked.shape[2]
    shaped = stacked.reshape(stacks, groups, 1, CAP, feature_width)
    spread_out = jnp.broadcast_to(shaped, (stacks, groups, GROUP, CAP, feature_width))
    return spread_out.reshape(stacks, groups * GROUP, CAP, feature_width)


def expert_forward(arriving, local_in, local_out):
    feature_width = arriving.shape[-1]
    preact = jnp.dot(
        arriving.reshape(-1, feature_width), local_in, preferred_element_type=jnp.float32
    )
    hidden = jax.nn.silu(preact).astype(jnp.bfloat16)
    partial_out = jnp.dot(hidden, local_out, preferred_element_type=jnp.float32).astype(
        jnp.bfloat16
    )
    return partial_out.reshape(arriving.shape)


def expert_backward(row_part, grad_part, local_in, local_out):
    feature_width = row_part.shape[-1]
    preact = jnp.dot(
        row_part.reshape(-1, feature_width), local_in, preferred_element_type=jnp.float32
    )
    sigmoid_v = jax.nn.sigmoid(preact)
    slope_v = sigmoid_v * (1.0 + preact * (1.0 - sigmoid_v))
    grad_hidden = jnp.einsum(
        "rd,hd->rh",
        grad_part.reshape(-1, feature_width),
        local_out,
        preferred_element_type=jnp.float32,
    )
    grad_pre = (grad_hidden * slope_v).astype(jnp.bfloat16)
    partial_grad = jnp.einsum(
        "rh,dh->rd", grad_pre, local_in, preferred_element_type=jnp.float32
    ).astype(jnp.bfloat16)
    return partial_grad.reshape(row_part.shape)


def gather_groups(returned, groups):
    feature_width = returned.shape[-1]
    summed = jnp.sum(
        returned.reshape(groups, GROUP, CAP, feature_width).astype(jnp.float32), axis=1
    )
    return summed.reshape(groups * CAP, feature_width)


def per_device(
    handoff,
    saved_inputs,
    cotangent,
    ids_forward,
    gates_forward,
    ids_backward,
    gates_backward,
    weight_in,
    weight_out,
):
    highest = lax.Precision.HIGHEST
    groups = lax.axis_size("expert") // GROUP
    segment_index = lax.axis_index("segment")
    last_segment = lax.axis_size("segment") - 1
    arrived = shifted(handoff, "segment", 1)
    inputs = jnp.where(segment_index == 0, handoff, arrived)[0]
    returned = shifted(cotangent, "segment", -1)
    upstream = jnp.where(segment_index == last_segment, cotangent, returned)[0]
    local_in = weight_in[0]
    local_out = weight_out[0]
    select_f, weigh_f = slot_tables(ids_forward[0], gates_forward[0], groups)
    picked = jnp.dot(
        select_f.astype(jnp.bfloat16), inputs, preferred_element_type=jnp.float32
    ).astype(jnp.bfloat16)
    select_b, weigh_b = slot_tables(ids_backward[0], gates_backward[0], groups)
    rows_back = jnp.dot(
        select_b.astype(jnp.bfloat16), saved_inputs[0], preferred_element_type=jnp.float32
    ).astype(jnp.bfloat16)
    grads_out = jnp.dot(
        weigh_b, upstream.astype(jnp.float32), precision=highest, preferred_element_type=jnp.float32
    ).astype(jnp.bfloat16)
    backward_stack = jnp.stack([rows_back, grads_out])
    arriving_f = lax.all_to_all(
        pack_direct(picked[None], groups), "expert", split_axis=1, concat_axis=1, tiled=True
    )
    arriving_b = lax.all_to_all(
        pack_direct(backward_stack, groups), "expert", split_axis=1, concat_axis=1, tiled=True
    )
    partial_f = expert_forward(arriving_f[0], local_in, local_out)
    back_f = lax.all_to_all(partial_f, "expert", split_axis=0, concat_axis=0, tiled=True)
    combined = gather_groups(back_f, groups)
    expert_mix = jnp.dot(
        weigh_f.T, combined, precision=highest, preferred_element_type=jnp.float32
    ).astype(jnp.bfloat16)
    partial_b = expert_backward(arriving_b[0], arriving_b[1], local_in, local_out)
    back_b = lax.all_to_all(partial_b, "expert", split_axis=0, concat_axis=0, tiled=True)
    slot_grads = gather_groups(back_b, groups)
    input_grads = jnp.dot(
        select_b.T, slot_grads, precision=highest, preferred_element_type=jnp.float32
    ).astype(jnp.bfloat16)
    return (expert_mix[None], input_grads[None])


MESH = pl.DeviceIdType.MESH
BLOCK = 16
HALF = 8
LANES = 128


def flipped(position, mask):
    bit = 1
    while bit <= mask:
        if mask & bit:
            position = position + bit * (1 - 2 * ((position // bit) % 2))
        bit *= 2
    return position


def exchange_kernel(
    planes,
    wire,
    ids_f_hbm,
    gates_f_hbm,
    ids_b_hbm,
    gates_b_hbm,
    handoff,
    saved,
    cotangent,
    weight_in,
    weight_out,
    out_f,
    out_b,
    rows_x,
    rows_s,
    w_in_side,
    w_out_side,
    blocks,
    req_send,
    req_recv,
    resp_send,
    resp_recv,
    own_rows,
    pair_send,
    pair_keep,
    pair_recv,
    y_send,
    y_keep,
    y_recv,
    z_send,
    z_recv,
    own_sum,
    ids_f,
    gates_f,
    ids_b,
    gates_b,
    scatter,
    gate_wide,
    local_sem,
    send_sem,
    recv_sem,
):
    segment = lax.axis_index("segment")
    expert = lax.axis_index("expert")
    row_count, width = rows_x.shape
    tail_width = width - wire
    hidden = weight_out.shape[0]

    def at_expert(mask):
        return {"expert": flipped(expert, mask)}

    other_segment = {"segment": 1 - segment}
    sibling = at_expert(1)
    across = at_expert(2)
    mates = [None] + [at_expert(4 * k) for k in range(1, planes)]

    barrier = pltpu.get_barrier_semaphore()
    partners = [other_segment, sibling, across] + mates[1:]
    for partner in partners:
        pl.semaphore_signal(barrier, inc=1, device_id=partner, device_id_type=MESH)

    tables = [
        pltpu.make_async_copy(source, target, local_sem.at[4 + i])
        for i, (source, target) in enumerate(
            [(ids_f_hbm, ids_f), (gates_f_hbm, gates_f), (ids_b_hbm, ids_b), (gates_b_hbm, gates_b)]
        )
    ]
    for table_copy in tables:
        table_copy.start()

    @pl.when(segment == 0)
    def _():
        pltpu.make_async_copy(handoff, rows_x, local_sem.at[0]).start()

    @pl.when(segment != 0)
    def _():
        pltpu.make_async_copy(cotangent, rows_x, local_sem.at[0]).start()

    load_x = pltpu.make_async_copy(handoff, rows_x, local_sem.at[0])
    load_s = pltpu.make_async_copy(saved, rows_s, local_sem.at[1])
    load_in = pltpu.make_async_copy(weight_in, w_in_side.at[:, 0:hidden], local_sem.at[2])
    load_out = pltpu.make_async_copy(weight_out, w_out_side.at[0:hidden, :], local_sem.at[3])
    load_s.start()
    load_in.start()
    load_out.start()

    count = [0]
    started = []

    def remote(source, target, device):
        number = count[0]
        count[0] += 1
        return pltpu.make_async_remote_copy(
            src_ref=source,
            dst_ref=target,
            send_sem=send_sem.at[number],
            recv_sem=recv_sem.at[number],
            device_id=device,
            device_id_type=MESH,
        )

    def begin(copy):
        copy.start()
        started.append(copy)

    plane = expert // 4
    order = [sorted(range(planes), key=lambda p: (abs(p - z), p)) for z in range(planes)]

    def on_plane(action):
        for z in range(planes):
            pl.when(plane == z)(functools.partial(action, z))

    def toward(z, p):
        return {"expert": expert + (p - z) * 4}

    request = remote(req_send, req_recv, other_segment)
    response = remote(resp_send, resp_recv, other_segment)
    gather_y = [remote(blocks.at[k, 0, 0], blocks.at[k, 1, 0], across) for k in range(planes)]
    gather_c0 = [remote(blocks.at[k, 0, 0], blocks.at[k, 0, 1], sibling) for k in range(planes)]
    gather_c1 = [remote(blocks.at[k, 1, 0], blocks.at[k, 1, 1], sibling) for k in range(planes)]
    reduce_c = [remote(pair_send.at[k], pair_recv.at[k], sibling) for k in range(planes)]
    reduce_y = [remote(y_send.at[k], y_recv.at[k], across) for k in range(planes)]
    gather_base, reduce_base = count[0], count[0] + planes + 1

    def gather_z(z, k, step):
        source = order[z][k]
        slot = order[z + step].index(source)
        number = gather_base + (planes if k == 0 and step > 0 else k)
        return pltpu.make_async_remote_copy(
            src_ref=blocks.at[k, 0, 0],
            dst_ref=blocks.at[slot, 0, 0],
            send_sem=send_sem.at[number],
            recv_sem=recv_sem.at[gather_base + slot],
            device_id=toward(z, z + step),
            device_id_type=MESH,
        )

    def onward(z, k):
        source = order[z][k]
        steps = [-1, 1] if source == z else [1 if source < z else -1]
        return [gather_z(z, k, step) for step in steps if 0 <= z + step < planes]

    def reduce_z(z, k):
        slot = order[order[z][k]].index(z)
        return pltpu.make_async_remote_copy(
            src_ref=z_send.at[k],
            dst_ref=z_recv.at[slot],
            send_sem=send_sem.at[reduce_base + k],
            recv_sem=recv_sem.at[reduce_base + slot],
            device_id=toward(z, order[z][k]),
            device_id_type=MESH,
        )

    def arrival(base, k, buffer):
        return pltpu.make_async_remote_copy(
            src_ref=buffer,
            dst_ref=buffer,
            send_sem=send_sem.at[base + k],
            recv_sem=recv_sem.at[base + k],
            device_id=sibling,
            device_id_type=MESH,
        )

    for table_copy in tables:
        table_copy.wait()
    earlier = jnp.where(
        lax.broadcasted_iota(jnp.int32, (row_count, row_count), 0)
        < lax.broadcasted_iota(jnp.int32, (row_count, row_count), 1),
        1.0,
        0.0,
    ).astype(jnp.bfloat16)

    def ranks(ids, gates):
        first, second = ids[0:1, :] == 0, ids[1:2, :] == 0
        member = jnp.where(first | second, 1.0, 0.0)
        gate = jnp.where(first, gates[0:1, :], 0.0) + jnp.where(second, gates[1:2, :], 0.0)
        wide = jnp.broadcast_to(member, (BLOCK, row_count))
        rank = jnp.dot(wide.astype(jnp.bfloat16), earlier, preferred_element_type=jnp.float32)
        return wide, rank.astype(jnp.int32), gate

    slot_row = lax.broadcasted_iota(jnp.int32, (BLOCK, row_count), 0)

    def placed(member, rank, offset):
        slot = slot_row - offset
        fits = (slot == rank) & (slot < CAP) & (slot >= 0)
        return jnp.where(fits, member, 0.0)

    member_f, rank_f, gate_f = ranks(ids_f, gates_f)
    member_b, rank_b, gate_b = ranks(ids_b, gates_b)
    later = (segment * jnp.ones((), jnp.int32)).astype(jnp.float32)
    first_f, first_b = placed(member_f, rank_f, 0), placed(member_b, rank_b, 0) * gate_b
    last_f, last_b = placed(member_f, rank_f, 2 * CAP), placed(member_b, rank_b, 2 * CAP) * gate_b
    asked = (first_b * (1.0 - later) + first_f * later)[0:HALF]
    mine = last_f * (1.0 - later) + last_b * later
    kept = placed(member_b, rank_b, CAP)
    req_send[...] = jnp.concatenate([asked, jnp.zeros((HALF, LANES - row_count), jnp.float32)], axis=1)
    pl.semaphore_wait(barrier, len(partners))
    begin(request)

    def picked(weights, rows_ref):
        scale = jnp.sum(weights, axis=1, keepdims=True)
        choose = jnp.where(weights != 0.0, 1.0, 0.0).astype(jnp.bfloat16)
        return jnp.dot(choose, rows_ref[...], preferred_element_type=jnp.float32) * scale

    load_x.wait()
    load_s.wait()
    own_rows[...] = picked(mine, rows_x) + picked(kept, rows_s)
    request.wait_recv()
    resp_send[...] = picked(req_recv[:, 0:row_count], rows_x).astype(jnp.bfloat16)
    begin(response)
    load_in.wait()
    load_out.wait()
    turn = 512 if width % 512 == 0 else LANES

    def transposes(step, carry):
        piece = pl.ds(pl.multiple_of(step * turn, turn), turn)
        w_in_side[piece, hidden : 2 * hidden] = w_out_side[0:hidden, piece].T
        w_out_side[hidden : 2 * hidden, piece] = w_in_side[piece, 0:hidden].T
        return carry

    lax.fori_loop(0, width // turn, transposes, 0)
    unit = jnp.where(
        lax.broadcasted_iota(jnp.int32, (row_count, row_count), 0)
        == lax.broadcasted_iota(jnp.int32, (row_count, row_count), 1),
        1.0,
        0.0,
    )
    by_row = (((1,), (1,)), ((), ()))
    for i, (member, rank, offset) in enumerate(
        [(member_f, rank_f, 0), (member_b, rank_b, CAP), (member_f, rank_f, 2 * CAP), (member_b, rank_b, 2 * CAP)]
    ):
        ones = placed(member, rank, offset)
        scatter[i] = lax.dot_general(
            unit.astype(jnp.bfloat16),
            jnp.concatenate([ones, ones], axis=0).astype(jnp.bfloat16),
            by_row,
            preferred_element_type=jnp.float32,
        ).astype(jnp.bfloat16)
    gate_wide[...] = lax.dot_general(
        unit,
        jnp.broadcast_to(gate_f, (LANES, row_count)),
        by_row,
        precision=lax.Precision.HIGHEST,
        preferred_element_type=jnp.float32,
    )
    response.wait_recv()
    own_rows[0:HALF, :] = own_rows[0:HALF, :] + resp_recv[...].astype(jnp.float32)
    blocks[0, 0, 0] = own_rows[...].astype(jnp.bfloat16)

    def spread(k):
        if k > 0:
            arrival(gather_base, k, blocks.at[k, 0, 0]).wait_recv()
        begin(gather_y[k])

        def pass_on(z):
            for copy in onward(z, k):
                copy.start()

        on_plane(pass_on)
        begin(gather_c0[k])

    def relay(k):
        gather_y[k].wait_recv()
        begin(gather_c1[k])

    batch = 4 * BLOCK
    place = lax.broadcasted_iota(jnp.int32, (batch, hidden), 0) % BLOCK
    chunk = 256 if tail_width % 256 == 0 and wire % 256 == 0 else LANES

    def compute(k):
        gather_c0[k].wait_recv()
        gather_c1[k].wait_recv()

        def contract(step, total):
            piece = pl.ds(pl.multiple_of(step * turn, turn), turn)
            return total + jnp.dot(
                blocks[k, :, :, :, piece].reshape(batch, turn),
                w_in_side[piece, :],
                preferred_element_type=jnp.float32,
            )

        both = lax.fori_loop(
            0, width // turn, contract, jnp.zeros((batch, 2 * hidden), jnp.float32), unroll=True
        )
        pre = both[:, 0:hidden]
        grad_hidden = both[:, hidden:]
        grad_hidden = (
            pltpu.roll(grad_hidden, CAP, 0) * (1.0 - later) + pltpu.roll(grad_hidden, batch - CAP, 0) * later
        )
        gate = 1.0 / (1.0 + jnp.exp(-pre))
        silu = pre * gate
        silu = pltpu.roll(silu, batch - 2 * CAP, 0) * (1.0 - later) + silu * later
        forward = jnp.where(place < CAP, silu, 0.0)
        slope = gate * (1.0 + pre * (1.0 - gate))
        backward = jnp.where((place >= CAP) & (place < 2 * CAP), grad_hidden * slope, 0.0)
        late_f = pltpu.roll(forward, 2 * CAP, 0).astype(jnp.bfloat16)
        late_b = pltpu.roll(backward, CAP, 0).astype(jnp.bfloat16)
        main = jnp.concatenate([forward, backward], axis=1).astype(jnp.bfloat16)

        def put(start, value):
            columns = pl.ds(start, chunk)
            value = value.reshape(2, 2, BLOCK, chunk)
            pair_keep[k, :, :, columns] = value[:, 0]
            pair_send[k, :, :, columns] = value[:, 1].astype(jnp.bfloat16)

        def product(start):
            return jnp.dot(main, w_out_side[:, pl.ds(start, chunk)], preferred_element_type=jnp.float32)

        def pieces(step, carry):
            start = pl.multiple_of(step * chunk, chunk)
            late = pl.ds(pl.multiple_of(wire + step * chunk, chunk), chunk)
            put(
                start,
                product(start)
                + jnp.dot(late_f, w_out_side[0:hidden, late], preferred_element_type=jnp.float32),
            )
            start = pl.multiple_of(tail_width + step * chunk, chunk)
            put(
                start,
                product(start)
                + jnp.dot(
                    late_b, w_out_side[hidden : 2 * hidden, late], preferred_element_type=jnp.float32
                ),
            )
            return carry

        lax.fori_loop(0, tail_width // chunk, pieces, 0, unroll=True)
        for start in range(2 * tail_width, wire, chunk):
            put(start, product(start))
        begin(reduce_c[k])

    def join_pair(k):
        reduce_c[k].wait_recv()
        y_send[k] = (pair_keep[k, 1] + pair_recv[k, 1].astype(jnp.float32)).astype(jnp.bfloat16)
        begin(reduce_y[k])
        y_keep[k] = pair_keep[k, 0] + pair_recv[k, 0].astype(jnp.float32)

    def join_plane(k):
        reduce_y[k].wait_recv()
        total = y_keep[k] + y_recv[k].astype(jnp.float32)
        if k == 0:
            own_sum[...] = total
        else:
            z_send[k] = total.astype(jnp.bfloat16)
            on_plane(lambda z: reduce_z(z, k).start())

    spread(0)
    for step in range(planes + 2):
        if step + 1 < planes:
            spread(step + 1)
        if step < planes:
            relay(step)
        if 0 <= step - 1 < planes:
            join_pair(step - 1)
        if 0 <= step - 2 < planes:
            join_plane(step - 2)
        if step < planes:
            compute(step)

    heads = scatter[0:2].reshape(2 * row_count, 2 * BLOCK)
    late_rows_f, late_rows_b = scatter[2], scatter[3]
    wide_gate = jnp.concatenate([gate_wide[...]] * (chunk // LANES), axis=1)
    for k in range(1, planes):
        arrival(reduce_base, k, z_recv.at[k]).wait_recv()

    def halves(start):
        columns = slice(start, start + chunk)
        total = own_sum[:, columns]
        for k in range(1, planes):
            total = total + z_recv[k, :, columns].astype(jnp.float32)
        high = total.astype(jnp.bfloat16)
        low = (total - high.astype(jnp.float32)).astype(jnp.bfloat16)
        return jnp.concatenate([high, low], axis=0)

    for start in range(0, wire, chunk):
        both = halves(start)
        value = jnp.dot(heads, both, preferred_element_type=jnp.float32)
        out_f[:, start : start + chunk] = (value[0:row_count] * wide_gate).astype(jnp.bfloat16)
        out_b[:, start : start + chunk] = value[row_count:].astype(jnp.bfloat16)
        if start < tail_width:
            value = jnp.dot(late_rows_f, both, preferred_element_type=jnp.float32) * wide_gate
            out_f[:, wire + start : wire + start + chunk] = value.astype(jnp.bfloat16)
        elif start < 2 * tail_width:
            late = wire + start - tail_width
            value = jnp.dot(late_rows_b, both, preferred_element_type=jnp.float32)
            out_b[:, late : late + chunk] = value.astype(jnp.bfloat16)
    for copy in started:
        copy.wait_send()

    def drain(z):
        for k in range(planes):
            for copy in onward(z, k):
                copy.wait_send()
            if k > 0:
                reduce_z(z, k).wait_send()

    on_plane(drain)


def exchange(planes, handoff, saved_inputs, cotangent, ids_forward, gates_forward, ids_backward, gates_backward, weight_in, weight_out):
    rows, width = handoff.shape[1:]
    hidden = weight_out.shape[1]
    tiles = width // LANES
    wire = -(-2 * tiles // 3) * LANES
    bf16, f32 = jnp.bfloat16, jnp.float32
    copies = 2 + 7 * planes + 1
    vmem = pl.BlockSpec(memory_space=pltpu.VMEM)
    hbm = pl.BlockSpec(memory_space=pl.ANY)
    mixed, grads = pl.pallas_call(
        functools.partial(exchange_kernel, planes, wire),
        out_shape=[jax.ShapeDtypeStruct((rows, width), bf16)] * 2,
        in_specs=[hbm] * 9,
        out_specs=[vmem] * 2,
        scratch_shapes=[
            pltpu.VMEM((rows, width), bf16),
            pltpu.VMEM((rows, width), bf16),
            pltpu.VMEM((width, 2 * hidden), bf16),
            pltpu.VMEM((2 * hidden, width), bf16),
            pltpu.VMEM((planes, 2, 2, BLOCK, width), bf16),
            pltpu.VMEM((HALF, LANES), f32),
            pltpu.VMEM((HALF, LANES), f32),
            pltpu.VMEM((HALF, width), bf16),
            pltpu.VMEM((HALF, width), bf16),
            pltpu.VMEM((BLOCK, width), f32),
            pltpu.VMEM((planes, 2, BLOCK, wire), bf16),
            pltpu.VMEM((planes, 2, BLOCK, wire), f32),
            pltpu.VMEM((planes, 2, BLOCK, wire), bf16),
            pltpu.VMEM((planes, BLOCK, wire), bf16),
            pltpu.VMEM((planes, BLOCK, wire), f32),
            pltpu.VMEM((planes, BLOCK, wire), bf16),
            pltpu.VMEM((planes, BLOCK, wire), bf16),
            pltpu.VMEM((planes, BLOCK, wire), bf16),
            pltpu.VMEM((BLOCK, wire), f32),
            pltpu.VMEM((2, rows), jnp.int32),
            pltpu.VMEM((2, rows), f32),
            pltpu.VMEM((2, rows), jnp.int32),
            pltpu.VMEM((2, rows), f32),
            pltpu.VMEM((4, rows, 2 * BLOCK), bf16),
            pltpu.VMEM((rows, LANES), f32),
            pltpu.SemaphoreType.DMA((8,)),
            pltpu.SemaphoreType.DMA((copies,)),
            pltpu.SemaphoreType.DMA((copies,)),
        ],
        compiler_params=pltpu.CompilerParams(
            collective_id=0, has_side_effects=True
        ),
    )(
        ids_forward[0].T,
        gates_forward[0].T,
        ids_backward[0].T,
        gates_backward[0].T,
        handoff[0],
        saved_inputs[0],
        cotangent[0],
        weight_in[0],
        weight_out[0],
    )
    return (mixed[None], grads[None])


def device_body(mesh):
    segments, experts = mesh.shape["segment"], mesh.shape["expert"]
    planes = experts // 4
    if segments == 2 and experts == GROUP and planes & (planes - 1) == 0:
        return functools.partial(exchange, planes)
    return per_device


def solution(mesh):
    return jax.shard_map(
        device_body(mesh),
        mesh=mesh,
        in_specs=(
            P("segment", "expert", None),
            P("segment", "expert", None),
            P("segment", "expert", None),
            P("segment", "expert", None),
            P("segment", "expert", None),
            P("segment", "expert", None),
            P("segment", "expert", None),
            P("segment", None, "expert"),
            P("segment", "expert", None),
        ),
        out_specs=(P("segment", "expert", None), P("segment", "expert", None)),
        check_vma=False,
    )
```

```python
import functools

import jax
import jax.numpy as jnp
from jax import lax
from jax.experimental import pallas as pl
from jax.experimental.pallas import tpu as pltpu
from jax.sharding import PartitionSpec as P

GROUP = 16
CAP = 5


def shifted(block, axis, distance):
    devices = range(lax.axis_size(axis))
    route = [(i - distance, i) for i in devices if i - distance in devices]
    return lax.ppermute(block, axis, route)


def slot_tables(expert_ids, gate_values, experts):
    row_count = expert_ids.shape[0]
    flat_ids = expert_ids.reshape(row_count * 2)
    window = jnp.arange(experts, dtype=jnp.int32)
    member = (flat_ids[None, :] == window[:, None]).astype(jnp.int32)
    before = jnp.cumsum(member, axis=1, dtype=jnp.int32) - member
    positions = jnp.arange(CAP, dtype=jnp.int32)
    picked_slots = (
        member[:, None, :] * (before[:, None, :] == positions[None, :, None]).astype(jnp.int32)
    ).astype(jnp.float32)
    picked_slots = picked_slots.reshape(experts * CAP, row_count, 2)
    select = jnp.sum(picked_slots, axis=2)
    weighted = jnp.sum(picked_slots * gate_values[None, :, :], axis=2)
    return (select, weighted)


def pack_direct(stacked, groups):
    stacks = stacked.shape[0]
    feature_width = stacked.shape[2]
    shaped = stacked.reshape(stacks, groups, 1, CAP, feature_width)
    spread_out = jnp.broadcast_to(shaped, (stacks, groups, GROUP, CAP, feature_width))
    return spread_out.reshape(stacks, groups * GROUP, CAP, feature_width)


def expert_forward(arriving, local_in, local_out):
    feature_width = arriving.shape[-1]
    preact = jnp.dot(
        arriving.reshape(-1, feature_width), local_in, preferred_element_type=jnp.float32
    )
    hidden = jax.nn.silu(preact).astype(jnp.bfloat16)
    partial_out = jnp.dot(hidden, local_out, preferred_element_type=jnp.float32).astype(
        jnp.bfloat16
    )
    return partial_out.reshape(arriving.shape)


def expert_backward(row_part, grad_part, local_in, local_out):
    feature_width = row_part.shape[-1]
    preact = jnp.dot(
        row_part.reshape(-1, feature_width), local_in, preferred_element_type=jnp.float32
    )
    sigmoid_v = jax.nn.sigmoid(preact)
    slope_v = sigmoid_v * (1.0 + preact * (1.0 - sigmoid_v))
    grad_hidden = jnp.einsum(
        "rd,hd->rh",
        grad_part.reshape(-1, feature_width),
        local_out,
        preferred_element_type=jnp.float32,
    )
    grad_pre = (grad_hidden * slope_v).astype(jnp.bfloat16)
    partial_grad = jnp.einsum(
        "rh,dh->rd", grad_pre, local_in, preferred_element_type=jnp.float32
    ).astype(jnp.bfloat16)
    return partial_grad.reshape(row_part.shape)


def gather_groups(returned, groups):
    feature_width = returned.shape[-1]
    summed = jnp.sum(
        returned.reshape(groups, GROUP, CAP, feature_width).astype(jnp.float32), axis=1
    )
    return summed.reshape(groups * CAP, feature_width)


def per_device(
    handoff,
    saved_inputs,
    cotangent,
    ids_forward,
    gates_forward,
    ids_backward,
    gates_backward,
    weight_in,
    weight_out,
):
    highest = lax.Precision.HIGHEST
    groups = lax.axis_size("expert") // GROUP
    segment_index = lax.axis_index("segment")
    last_segment = lax.axis_size("segment") - 1
    arrived = shifted(handoff, "segment", 1)
    inputs = jnp.where(segment_index == 0, handoff, arrived)[0]
    returned = shifted(cotangent, "segment", -1)
    upstream = jnp.where(segment_index == last_segment, cotangent, returned)[0]
    local_in = weight_in[0]
    local_out = weight_out[0]
    select_f, weigh_f = slot_tables(ids_forward[0], gates_forward[0], groups)
    picked = jnp.dot(
        select_f.astype(jnp.bfloat16), inputs, preferred_element_type=jnp.float32
    ).astype(jnp.bfloat16)
    select_b, weigh_b = slot_tables(ids_backward[0], gates_backward[0], groups)
    rows_back = jnp.dot(
        select_b.astype(jnp.bfloat16), saved_inputs[0], preferred_element_type=jnp.float32
    ).astype(jnp.bfloat16)
    grads_out = jnp.dot(
        weigh_b, upstream.astype(jnp.float32), precision=highest, preferred_element_type=jnp.float32
    ).astype(jnp.bfloat16)
    backward_stack = jnp.stack([rows_back, grads_out])
    arriving_f = lax.all_to_all(
        pack_direct(picked[None], groups), "expert", split_axis=1, concat_axis=1, tiled=True
    )
    arriving_b = lax.all_to_all(
        pack_direct(backward_stack, groups), "expert", split_axis=1, concat_axis=1, tiled=True
    )
    partial_f = expert_forward(arriving_f[0], local_in, local_out)
    back_f = lax.all_to_all(partial_f, "expert", split_axis=0, concat_axis=0, tiled=True)
    combined = gather_groups(back_f, groups)
    expert_mix = jnp.dot(
        weigh_f.T, combined, precision=highest, preferred_element_type=jnp.float32
    ).astype(jnp.bfloat16)
    partial_b = expert_backward(arriving_b[0], arriving_b[1], local_in, local_out)
    back_b = lax.all_to_all(partial_b, "expert", split_axis=0, concat_axis=0, tiled=True)
    slot_grads = gather_groups(back_b, groups)
    input_grads = jnp.dot(
        select_b.T, slot_grads, precision=highest, preferred_element_type=jnp.float32
    ).astype(jnp.bfloat16)
    return (expert_mix[None], input_grads[None])


MESH = pl.DeviceIdType.MESH
BLOCK = 16
HALF = 8
PARTS = 2
LANES = 128


def flipped(position, mask):
    bit = 1
    while bit <= mask:
        if mask & bit:
            position = position + bit * (1 - 2 * ((position // bit) % 2))
        bit *= 2
    return position


def exchange_kernel(
    planes,
    wire,
    ids_f_hbm,
    gates_f_hbm,
    ids_b_hbm,
    gates_b_hbm,
    handoff,
    saved,
    cotangent,
    weight_in,
    weight_out,
    out_f,
    out_b,
    rows_x,
    rows_s,
    w_in_side,
    w_out_side,
    blocks,
    req_send,
    req_recv,
    resp_send,
    resp_recv,
    own_rows,
    pair_send,
    pair_keep,
    pair_recv,
    y_send,
    y_keep,
    y_recv,
    z_send,
    z_recv,
    own_sum,
    ids_f,
    gates_f,
    ids_b,
    gates_b,
    scatter,
    gate_wide,
    local_sem,
    send_sem,
    recv_sem,
):
    segment = lax.axis_index("segment")
    expert = lax.axis_index("expert")
    row_count, width = rows_x.shape
    tail_width = width - wire
    hidden = weight_out.shape[0]

    def at_expert(mask):
        return {"expert": flipped(expert, mask)}

    other_segment = {"segment": 1 - segment}
    sibling = at_expert(1)
    across = at_expert(2)
    mates = [None] + [at_expert(4 * k) for k in range(1, planes)]

    barrier = pltpu.get_barrier_semaphore()
    partners = [other_segment, sibling, across] + mates[1:]
    for partner in partners:
        pl.semaphore_signal(barrier, inc=1, device_id=partner, device_id_type=MESH)

    tables = [
        pltpu.make_async_copy(source, target, local_sem.at[4 + i])
        for i, (source, target) in enumerate(
            [(ids_f_hbm, ids_f), (gates_f_hbm, gates_f), (ids_b_hbm, ids_b), (gates_b_hbm, gates_b)]
        )
    ]
    for table_copy in tables:
        table_copy.start()

    @pl.when(segment == 0)
    def _():
        pltpu.make_async_copy(handoff, rows_x, local_sem.at[0]).start()

    @pl.when(segment != 0)
    def _():
        pltpu.make_async_copy(cotangent, rows_x, local_sem.at[0]).start()

    load_x = pltpu.make_async_copy(handoff, rows_x, local_sem.at[0])
    load_s = pltpu.make_async_copy(saved, rows_s, local_sem.at[1])
    load_in = pltpu.make_async_copy(weight_in, w_in_side.at[:, 0:hidden], local_sem.at[2])
    load_out = pltpu.make_async_copy(weight_out, w_out_side.at[0:hidden, :], local_sem.at[3])
    load_s.start()
    load_in.start()
    load_out.start()

    count = [0]
    started = []

    def remote(source, target, device):
        number = count[0]
        count[0] += 1
        return pltpu.make_async_remote_copy(
            src_ref=source,
            dst_ref=target,
            send_sem=send_sem.at[number],
            recv_sem=recv_sem.at[number],
            device_id=device,
            device_id_type=MESH,
        )

    def begin(copy):
        copy.start()
        started.append(copy)

    request = remote(req_send, req_recv, other_segment)
    response = remote(resp_send, resp_recv, other_segment)

    def cuts(total):
        tiles = total // LANES
        edges = [tiles * i // PARTS * LANES for i in range(PARTS + 1)]
        return [slice(low, high) for low, high in zip(edges[:-1], edges[1:])]

    wide_cuts, wire_cuts = cuts(width), cuts(wire)

    def gather(source, target, device):
        return [
            remote(blocks.at[(*source, slice(None), cut)], blocks.at[(*target, slice(None), cut)], device)
            for cut in wide_cuts
        ]

    gather_z = [None] + [gather((0, 0, 0), (k, 0, 0), mates[k]) for k in range(1, planes)]
    gather_y = [gather((k, 0, 0), (k, 1, 0), across) for k in range(planes)]
    gather_c0 = [gather((k, 0, 0), (k, 0, 1), sibling) for k in range(planes)]
    gather_c1 = [gather((k, 1, 0), (k, 1, 1), sibling) for k in range(planes)]
    reduce_c = [
        [remote(pair_send.at[k, :, :, cut], pair_recv.at[k, :, :, cut], sibling) for cut in wire_cuts]
        for k in range(planes)
    ]
    reduce_y = [
        [remote(y_send.at[k, :, cut], y_recv.at[k, :, cut], across) for cut in wire_cuts]
        for k in range(planes)
    ]
    reduce_z = [None] + [
        [remote(z_send.at[k, :, cut], z_recv.at[k, :, cut], mates[k]) for cut in wire_cuts]
        for k in range(1, planes)
    ]

    for table_copy in tables:
        table_copy.wait()
    earlier = jnp.where(
        lax.broadcasted_iota(jnp.int32, (row_count, row_count), 0)
        < lax.broadcasted_iota(jnp.int32, (row_count, row_count), 1),
        1.0,
        0.0,
    ).astype(jnp.bfloat16)

    def ranks(ids, gates):
        first, second = ids[0:1, :] == 0, ids[1:2, :] == 0
        member = jnp.where(first | second, 1.0, 0.0)
        gate = jnp.where(first, gates[0:1, :], 0.0) + jnp.where(second, gates[1:2, :], 0.0)
        wide = jnp.broadcast_to(member, (BLOCK, row_count))
        rank = jnp.dot(wide.astype(jnp.bfloat16), earlier, preferred_element_type=jnp.float32)
        return wide, rank.astype(jnp.int32), gate

    slot_row = lax.broadcasted_iota(jnp.int32, (BLOCK, row_count), 0)

    def placed(member, rank, offset):
        slot = slot_row - offset
        fits = (slot == rank) & (slot < CAP) & (slot >= 0)
        return jnp.where(fits, member, 0.0)

    member_f, rank_f, gate_f = ranks(ids_f, gates_f)
    member_b, rank_b, gate_b = ranks(ids_b, gates_b)
    later = (segment * jnp.ones((), jnp.int32)).astype(jnp.float32)
    first_f, first_b = placed(member_f, rank_f, 0), placed(member_b, rank_b, 0) * gate_b
    last_f, last_b = placed(member_f, rank_f, 2 * CAP), placed(member_b, rank_b, 2 * CAP) * gate_b
    asked = (first_b * (1.0 - later) + first_f * later)[0:HALF]
    mine = last_f * (1.0 - later) + last_b * later
    kept = placed(member_b, rank_b, CAP)
    req_send[...] = jnp.concatenate([asked, jnp.zeros((HALF, LANES - row_count), jnp.float32)], axis=1)
    pl.semaphore_wait(barrier, len(partners))
    begin(request)

    def picked(weights, rows_ref):
        scale = jnp.sum(weights, axis=1, keepdims=True)
        choose = jnp.where(weights != 0.0, 1.0, 0.0).astype(jnp.bfloat16)
        return jnp.dot(choose, rows_ref[...], preferred_element_type=jnp.float32) * scale

    load_x.wait()
    load_s.wait()
    own_rows[...] = picked(mine, rows_x) + picked(kept, rows_s)
    request.wait_recv()
    resp_send[...] = picked(req_recv[:, 0:row_count], rows_x).astype(jnp.bfloat16)
    begin(response)
    load_in.wait()
    load_out.wait()
    turn = 512 if width % 512 == 0 else LANES

    def transposes(step, carry):
        piece = pl.ds(pl.multiple_of(step * turn, turn), turn)
        w_in_side[piece, hidden : 2 * hidden] = w_out_side[0:hidden, piece].T
        w_out_side[hidden : 2 * hidden, piece] = w_in_side[piece, 0:hidden].T
        return carry

    lax.fori_loop(0, width // turn, transposes, 0)
    unit = jnp.where(
        lax.broadcasted_iota(jnp.int32, (row_count, row_count), 0)
        == lax.broadcasted_iota(jnp.int32, (row_count, row_count), 1),
        1.0,
        0.0,
    )
    by_row = (((1,), (1,)), ((), ()))
    for i, (member, rank, offset) in enumerate(
        [(member_f, rank_f, 0), (member_b, rank_b, CAP), (member_f, rank_f, 2 * CAP), (member_b, rank_b, 2 * CAP)]
    ):
        ones = placed(member, rank, offset)
        scatter[i] = lax.dot_general(
            unit.astype(jnp.bfloat16),
            jnp.concatenate([ones, ones], axis=0).astype(jnp.bfloat16),
            by_row,
            preferred_element_type=jnp.float32,
        ).astype(jnp.bfloat16)
    gate_wide[...] = lax.dot_general(
        unit,
        jnp.broadcast_to(gate_f, (LANES, row_count)),
        by_row,
        precision=lax.Precision.HIGHEST,
        preferred_element_type=jnp.float32,
    )
    response.wait_recv()
    own_rows[0:HALF, :] = own_rows[0:HALF, :] + resp_recv[...].astype(jnp.float32)
    blocks[0, 0, 0] = own_rows[...].astype(jnp.bfloat16)

    def spread(k):
        for part in range(PARTS):
            if k > 0:
                gather_z[k][part].wait_recv()
            begin(gather_y[k][part])
            begin(gather_c0[k][part])

    def relay(k):
        for part in range(PARTS):
            gather_y[k][part].wait_recv()
            begin(gather_c1[k][part])

    batch = 4 * BLOCK
    place = lax.broadcasted_iota(jnp.int32, (batch, hidden), 0) % BLOCK
    chunk = 256 if tail_width % 256 == 0 and wire % 256 == 0 else LANES

    def compute(k):
        for part in range(PARTS):
            gather_c0[k][part].wait_recv()
            gather_c1[k][part].wait_recv()

        def contract(step, total):
            piece = pl.ds(pl.multiple_of(step * turn, turn), turn)
            return total + jnp.dot(
                blocks[k, :, :, :, piece].reshape(batch, turn),
                w_in_side[piece, :],
                preferred_element_type=jnp.float32,
            )

        both = lax.fori_loop(
            0, width // turn, contract, jnp.zeros((batch, 2 * hidden), jnp.float32), unroll=True
        )
        pre = both[:, 0:hidden]
        grad_hidden = both[:, hidden:]
        grad_hidden = (
            pltpu.roll(grad_hidden, CAP, 0) * (1.0 - later) + pltpu.roll(grad_hidden, batch - CAP, 0) * later
        )
        gate = 1.0 / (1.0 + jnp.exp(-pre))
        silu = pre * gate
        silu = pltpu.roll(silu, batch - 2 * CAP, 0) * (1.0 - later) + silu * later
        forward = jnp.where(place < CAP, silu, 0.0)
        slope = gate * (1.0 + pre * (1.0 - gate))
        backward = jnp.where((place >= CAP) & (place < 2 * CAP), grad_hidden * slope, 0.0)
        late_f = pltpu.roll(forward, 2 * CAP, 0).astype(jnp.bfloat16)
        late_b = pltpu.roll(backward, CAP, 0).astype(jnp.bfloat16)
        main = jnp.concatenate([forward, backward], axis=1).astype(jnp.bfloat16)

        def put(start, value):
            columns = pl.ds(start, chunk)
            value = value.reshape(2, 2, BLOCK, chunk)
            pair_keep[k, :, :, columns] = value[:, 0]
            pair_send[k, :, :, columns] = value[:, 1].astype(jnp.bfloat16)

        def product(start):
            return jnp.dot(main, w_out_side[:, pl.ds(start, chunk)], preferred_element_type=jnp.float32)

        def pieces(step, carry):
            start = pl.multiple_of(step * chunk, chunk)
            late = pl.ds(pl.multiple_of(wire + step * chunk, chunk), chunk)
            put(
                start,
                product(start)
                + jnp.dot(late_f, w_out_side[0:hidden, late], preferred_element_type=jnp.float32),
            )
            start = pl.multiple_of(tail_width + step * chunk, chunk)
            put(
                start,
                product(start)
                + jnp.dot(
                    late_b, w_out_side[hidden : 2 * hidden, late], preferred_element_type=jnp.float32
                ),
            )
            return carry

        lax.fori_loop(0, tail_width // chunk, pieces, 0, unroll=True)
        for start in range(2 * tail_width, wire, chunk):
            put(start, product(start))
        for copy in reduce_c[k]:
            begin(copy)

    def join_pair(k):
        for part, cut in enumerate(wire_cuts):
            reduce_c[k][part].wait_recv()
            sent = pair_keep[k, 1, :, cut] + pair_recv[k, 1, :, cut].astype(jnp.float32)
            y_send[k, :, cut] = sent.astype(jnp.bfloat16)
            begin(reduce_y[k][part])
            y_keep[k, :, cut] = pair_keep[k, 0, :, cut] + pair_recv[k, 0, :, cut].astype(jnp.float32)

    def join_plane(k):
        for part, cut in enumerate(wire_cuts):
            reduce_y[k][part].wait_recv()
            total = y_keep[k, :, cut] + y_recv[k, :, cut].astype(jnp.float32)
            if k == 0:
                own_sum[:, cut] = total
            else:
                z_send[k, :, cut] = total.astype(jnp.bfloat16)
                begin(reduce_z[k][part])

    for k in range(1, planes):
        for copy in gather_z[k]:
            begin(copy)
    spread(0)
    last = planes - 1
    for step in range(last):
        spread(step + 1)
        if step == last - 1:
            for k in range(step):
                join_pair(k)
        relay(step)
        compute(step)
    join_pair(last - 1)
    relay(last)
    join_plane(0)
    compute(last)
    join_pair(last)
    for k in range(1, planes):
        join_plane(k)

    heads = scatter[0:2].reshape(2 * row_count, 2 * BLOCK)
    late_rows_f, late_rows_b = scatter[2], scatter[3]
    wide_gate = jnp.concatenate([gate_wide[...]] * (chunk // LANES), axis=1)
    for k in range(1, planes):
        for copy in reduce_z[k]:
            copy.wait_recv()

    def halves(start):
        columns = slice(start, start + chunk)
        total = own_sum[:, columns]
        for k in range(1, planes):
            total = total + z_recv[k, :, columns].astype(jnp.float32)
        high = total.astype(jnp.bfloat16)
        low = (total - high.astype(jnp.float32)).astype(jnp.bfloat16)
        return jnp.concatenate([high, low], axis=0)

    for start in range(0, wire, chunk):
        both = halves(start)
        value = jnp.dot(heads, both, preferred_element_type=jnp.float32)
        out_f[:, start : start + chunk] = (value[0:row_count] * wide_gate).astype(jnp.bfloat16)
        out_b[:, start : start + chunk] = value[row_count:].astype(jnp.bfloat16)
        if start < tail_width:
            value = jnp.dot(late_rows_f, both, preferred_element_type=jnp.float32) * wide_gate
            out_f[:, wire + start : wire + start + chunk] = value.astype(jnp.bfloat16)
        elif start < 2 * tail_width:
            late = wire + start - tail_width
            value = jnp.dot(late_rows_b, both, preferred_element_type=jnp.float32)
            out_b[:, late : late + chunk] = value.astype(jnp.bfloat16)
    for copy in started:
        copy.wait_send()


def exchange(planes, handoff, saved_inputs, cotangent, ids_forward, gates_forward, ids_backward, gates_backward, weight_in, weight_out):
    rows, width = handoff.shape[1:]
    hidden = weight_out.shape[1]
    tiles = width // LANES
    wire = -(-2 * tiles // 3) * LANES
    bf16, f32 = jnp.bfloat16, jnp.float32
    copies = 2 + PARTS * (2 * (planes - 1) + 5 * planes)
    vmem = pl.BlockSpec(memory_space=pltpu.VMEM)
    hbm = pl.BlockSpec(memory_space=pl.ANY)
    mixed, grads = pl.pallas_call(
        functools.partial(exchange_kernel, planes, wire),
        out_shape=[jax.ShapeDtypeStruct((rows, width), bf16)] * 2,
        in_specs=[hbm] * 9,
        out_specs=[vmem] * 2,
        scratch_shapes=[
            pltpu.VMEM((rows, width), bf16),
            pltpu.VMEM((rows, width), bf16),
            pltpu.VMEM((width, 2 * hidden), bf16),
            pltpu.VMEM((2 * hidden, width), bf16),
            pltpu.VMEM((planes, 2, 2, BLOCK, width), bf16),
            pltpu.VMEM((HALF, LANES), f32),
            pltpu.VMEM((HALF, LANES), f32),
            pltpu.VMEM((HALF, width), bf16),
            pltpu.VMEM((HALF, width), bf16),
            pltpu.VMEM((BLOCK, width), f32),
            pltpu.VMEM((planes, 2, BLOCK, wire), bf16),
            pltpu.VMEM((planes, 2, BLOCK, wire), f32),
            pltpu.VMEM((planes, 2, BLOCK, wire), bf16),
            pltpu.VMEM((planes, BLOCK, wire), bf16),
            pltpu.VMEM((planes, BLOCK, wire), f32),
            pltpu.VMEM((planes, BLOCK, wire), bf16),
            pltpu.VMEM((planes, BLOCK, wire), bf16),
            pltpu.VMEM((planes, BLOCK, wire), bf16),
            pltpu.VMEM((BLOCK, wire), f32),
            pltpu.VMEM((2, rows), jnp.int32),
            pltpu.VMEM((2, rows), f32),
            pltpu.VMEM((2, rows), jnp.int32),
            pltpu.VMEM((2, rows), f32),
            pltpu.VMEM((4, rows, 2 * BLOCK), bf16),
            pltpu.VMEM((rows, LANES), f32),
            pltpu.SemaphoreType.DMA((8,)),
            pltpu.SemaphoreType.DMA((copies,)),
            pltpu.SemaphoreType.DMA((copies,)),
        ],
        compiler_params=pltpu.CompilerParams(
            collective_id=0, has_side_effects=True
        ),
    )(
        ids_forward[0].T,
        gates_forward[0].T,
        ids_backward[0].T,
        gates_backward[0].T,
        handoff[0],
        saved_inputs[0],
        cotangent[0],
        weight_in[0],
        weight_out[0],
    )
    return (mixed[None], grads[None])


def device_body(mesh):
    segments, experts = mesh.shape["segment"], mesh.shape["expert"]
    planes = experts // 4
    if segments == 2 and experts == GROUP and planes & (planes - 1) == 0:
        return functools.partial(exchange, planes)
    return per_device


def solution(mesh):
    return jax.shard_map(
        device_body(mesh),
        mesh=mesh,
        in_specs=(
            P("segment", "expert", None),
            P("segment", "expert", None),
            P("segment", "expert", None),
            P("segment", "expert", None),
            P("segment", "expert", None),
            P("segment", "expert", None),
            P("segment", "expert", None),
            P("segment", None, "expert"),
            P("segment", "expert", None),
        ),
        out_specs=(P("segment", "expert", None), P("segment", "expert", None)),
        check_vma=False,
    )
```
